256 devices in a mesh: seq: 64 (over x, z, core), head: 4 (over y).
Axes of the slice: x: 4, y: 4, z: 8, core: 2. Of those that a mesh axis runs over, the one named last changes fastest.
Arguments:
- queries: bfloat16 [16384, 8192], P('seq', 'head'), may hold values from -200 to 200
- keys: bfloat16 [16384, 1024], P('seq', 'head'), may hold values from -6 to 6
- values: bfloat16 [16384, 1024], P('seq', 'head'), may hold values from -6 to 6
- output_gradient: bfloat16 [16384, 8192], P('seq', 'head'), may hold values from -6 to 6
- lengths: int32 [32], replicated, may hold values from 1 to 1024, 16384 in all
Outputs:
- attn_out: bfloat16 [16384, 8192], P(('seq', 'head'))
- d_queries: bfloat16 [16384, 8192], P('seq', 'head')
- key_gradient: bfloat16 [16384, 1024], P('seq', 'head')
- value_gradient: bfloat16 [16384, 1024], P('seq', 'head')
The draws below stay inside these ranges and needn't reach their ends.
Inputs may be any that keep to these rules, and one draw needn't show every extreme that they name: 32 lengths that sum to 16384; the longest is exactly 1024.
All inputs are finite; a program needn't handle non-finite values.
Results may differ from the reference program's by a relative error of at most 0.035.
Values may be sent and summed in bfloat16 or wider, within the bound.
No kernel may reach another device: no remote copies, remote signals or barrier semaphores. Data moves between devices by JAX's collectives and lax.ppermute only.
A program may use at most 128 MiB of HBM per device.

```python
import math
import jax
import jax.numpy as jnp
import numpy as np
from jax import lax

QUERY_HEADS = 64
KEY_VALUE_HEADS = 8
HEAD_WIDTH = 128
TOK_SEQ = 256
PACKED_TOKENS = 16384
LONGEST_DOC = 1024
DOCS = 32


def drawn_pair(key):
    unshaped_keys = jax.random.truncated_normal(jax.random.fold_in(key, 11), -6.0, 6.0, (PACKED_TOKENS, KEY_VALUE_HEADS, HEAD_WIDTH), jnp.float32)
    queries_raw = jax.random.truncated_normal(jax.random.fold_in(key, 12), -6.0, 6.0, (PACKED_TOKENS, QUERY_HEADS, HEAD_WIDTH), jnp.float32)
    return (queries_raw, unshaped_keys)


def draw_queries(key, part):
    queries_raw, unshaped_keys = drawn_pair(key)
    return queries_raw.reshape(PACKED_TOKENS, QUERY_HEADS * HEAD_WIDTH).astype(jnp.bfloat16)


def draw_keys(key, part):
    queries_raw, unshaped_keys = drawn_pair(key)
    return unshaped_keys.reshape(PACKED_TOKENS, KEY_VALUE_HEADS * HEAD_WIDTH).astype(jnp.bfloat16)


def levels(key, extent, shards, least, top_value):
    def one(dim, shards_of):
        heights = jax.random.uniform(jax.random.fold_in(jax.random.fold_in(key, 6), dim), (shards_of,), jnp.float32, least / len(shards), top_value / len(shards))
        return jnp.repeat(jnp.exp(heights), extent[dim] // shards_of).reshape((-1,) + (1,) * (len(extent) - dim - 1))

    factor_of = one(*shards[0])
    for cut in shards[1:]:
        factor_of = factor_of * one(*cut)
    return factor_of


def profile(number_of, total, most, lean):
    loads = [(1 << 20) // math.isqrt(rank ** lean) + 1 for rank in range(2, number_of + 1)]
    surplus, counts = total - most - (number_of - 1), [1] * (number_of - 1)
    while surplus > 0:
        free = [i for i in range(number_of - 1) if counts[i] < most]
        pool, remaining = sum([loads[i] for i in free]), surplus
        for i in free:
            more = min(most - counts[i], max(1, remaining * loads[i] // pool), surplus)
            counts[i] = counts[i] + more
            surplus = surplus - more
    return np.array([most] + counts)


def uneven(key, amount, total, most, lean):
    if amount == 2:
        one = jax.random.randint(key, (), max(1, total - most), min(most, total - 1) + 1)
        return jnp.stack([one, total - one])
    sizes = jnp.asarray(profile(amount, total, most, lean), jnp.int32)
    twos = (amount - 1) // 2
    giver, taker = sizes[1:1 + 2 * twos:2], sizes[2:2 + 2 * twos:2]
    slack = jnp.minimum(giver - 1, most - taker)
    shifted = jax.random.randint(jax.random.fold_in(key, 1), (twos,), 0, 1 << 20) % (slack + 1)
    sizes = sizes.at[1:1 + 2 * twos:2].set(giver - shifted).at[2:2 + 2 * twos:2].set(taker + shifted)
    return sizes[jax.random.permutation(jax.random.fold_in(key, 2), amount)]


def noise(stream_key, extent, spread, reach, shards=(), kind=jnp.bfloat16):
    entries = spread * jax.random.normal(stream_key, extent, jnp.float32)
    if shards:
        entries = entries * levels(stream_key, extent, shards, -0.22, 0.18)
    return jnp.clip(entries, -reach, reach).astype(kind)


def setup_inputs(seed: int = 0) -> dict:
    arg_keys = jax.random.split(jax.random.key(seed), 6)
    return {
        "queries": draw_queries(jax.random.fold_in(arg_keys[5], 71), 0),
        "keys": draw_keys(jax.random.fold_in(arg_keys[5], 71), 0),
        "values": noise(arg_keys[2], (PACKED_TOKENS, KEY_VALUE_HEADS * HEAD_WIDTH), 1.0, 6.0, ((0, 64), (1, 4))),
        "output_gradient": noise(arg_keys[3], (PACKED_TOKENS, QUERY_HEADS * HEAD_WIDTH), 1.0, 6.0, ((0, 64), (1, 4))),
        "lengths": uneven(arg_keys[4], DOCS, PACKED_TOKENS, LONGEST_DOC, 2).astype(jnp.int32),
    }


def doc_numbers(positions, ends):
    return lax.optimization_barrier(jnp.sum((positions[:, None] >= ends[None, :]).astype(jnp.int32), axis=1))

def reference(queries, keys, values, output_gradient, lengths):
    scale = 1.0 / math.sqrt(HEAD_WIDTH)
    query_group = QUERY_HEADS // KEY_VALUE_HEADS
    ends = jnp.cumsum(lengths).astype(jnp.int32)
    width = LONGEST_DOC + TOK_SEQ
    query_tensor_four = queries.reshape(PACKED_TOKENS, KEY_VALUE_HEADS, query_group, HEAD_WIDTH)
    output_cotangent = output_gradient.reshape(PACKED_TOKENS, KEY_VALUE_HEADS, query_group, HEAD_WIDTH)
    blank_rows = jnp.zeros((LONGEST_DOC, KEY_VALUE_HEADS * HEAD_WIDTH), keys.dtype)
    key_tensor_three = jnp.concatenate([blank_rows, keys], axis=0).reshape(LONGEST_DOC + PACKED_TOKENS, KEY_VALUE_HEADS, HEAD_WIDTH)
    value_tensor_three = jnp.concatenate([blank_rows, values], axis=0).reshape(LONGEST_DOC + PACKED_TOKENS, KEY_VALUE_HEADS, HEAD_WIDTH)
    offsets = jnp.arange(TOK_SEQ, dtype=jnp.int32)
    window = jnp.arange(width, dtype=jnp.int32)

    def one_block(carry, index):
        key_gradient_sum, value_gradient_sum = carry
        start = (index * TOK_SEQ).astype(jnp.int32)
        query_pos = start + offsets
        key_pos = start - LONGEST_DOC + window
        allowed = doc_numbers(query_pos, ends)[:, None] == doc_numbers(key_pos, ends)[None, :]
        allowed = allowed & (key_pos[None, :] >= 0) & (key_pos[None, :] <= query_pos[:, None])
        q_block = lax.dynamic_slice_in_dim(query_tensor_four, start, TOK_SEQ, 0).astype(jnp.float32)
        d_block = lax.dynamic_slice_in_dim(output_cotangent, start, TOK_SEQ, 0).astype(jnp.float32)
        k_block = lax.dynamic_slice_in_dim(key_tensor_three, start, width, 0).astype(jnp.float32)
        v_block = lax.dynamic_slice_in_dim(value_tensor_three, start, width, 0).astype(jnp.float32)
        scores = jnp.einsum('qhgd,khd->hgqk', q_block, k_block) * scale
        scores = jnp.where(allowed[None, None], scores, -jnp.inf)
        top = lax.optimization_barrier(jnp.max(scores, axis=-1))
        lse = top + jnp.log(lax.optimization_barrier(jnp.sum(jnp.exp(scores - top[..., None]), axis=-1)))
        probs = jnp.exp(scores - lse[..., None])
        probs_b = lax.optimization_barrier(probs.astype(jnp.bfloat16)).astype(jnp.float32)
        out_block = jnp.einsum('hgqk,khd->qhgd', probs_b, v_block).astype(jnp.bfloat16)
        out_wide = lax.optimization_barrier(out_block).astype(jnp.float32)
        delta = jnp.transpose(lax.optimization_barrier(jnp.sum(d_block * out_wide, axis=-1)), (1, 2, 0))
        dprobs = jnp.einsum('qhgd,khd->hgqk', d_block, v_block)
        dscores = (probs * (dprobs - delta[..., None])).astype(jnp.bfloat16)
        dscores = lax.optimization_barrier(dscores).astype(jnp.float32)
        dq_block = (jnp.einsum('hgqk,khd->qhgd', dscores, k_block) * scale).astype(jnp.bfloat16)
        dk_window = jnp.einsum('hgqk,qhgd->khd', dscores, q_block) * scale
        dv_window = jnp.einsum('hgqk,qhgd->khd', probs_b, d_block)
        key_gradient_sum = lax.dynamic_update_slice_in_dim(key_gradient_sum, lax.dynamic_slice_in_dim(key_gradient_sum, start, width, 0) + dk_window, start, 0)
        value_gradient_sum = lax.dynamic_update_slice_in_dim(value_gradient_sum, lax.dynamic_slice_in_dim(value_gradient_sum, start, width, 0) + dv_window, start, 0)
        return ((key_gradient_sum, value_gradient_sum), (out_block, dq_block))
    blank_accumulator = jnp.zeros((LONGEST_DOC + PACKED_TOKENS, KEY_VALUE_HEADS, HEAD_WIDTH), jnp.float32)
    (key_gradient_sum, value_gradient_sum), (outs, dqs) = lax.scan(one_block, (blank_accumulator, blank_accumulator), jnp.arange(PACKED_TOKENS // TOK_SEQ, dtype=jnp.int32))
    attn_out = outs.reshape(PACKED_TOKENS, QUERY_HEADS * HEAD_WIDTH)
    d_queries = dqs.reshape(PACKED_TOKENS, QUERY_HEADS * HEAD_WIDTH)
    key_gradient = key_gradient_sum[LONGEST_DOC:].reshape(PACKED_TOKENS, KEY_VALUE_HEADS * HEAD_WIDTH).astype(jnp.bfloat16)
    value_gradient = value_gradient_sum[LONGEST_DOC:].reshape(PACKED_TOKENS, KEY_VALUE_HEADS * HEAD_WIDTH).astype(jnp.bfloat16)
    return (attn_out, d_queries, key_gradient, value_gradient)
```

```python
import functools
import math

import jax
import jax.numpy as jnp
from jax import lax
from jax.experimental import pallas as pl
from jax.experimental.pallas import tpu as pltpu
from jax.sharding import PartitionSpec as P

HEAD_WIDTH = 128
REACH = 4
NEG = -1e30
LOG2E = 1.4426950408889634
HEADS_PER_STEP = 4


def dot(a, b):
    return lax.dot_general(a, b, (((1,), (0,)), ((), ())), preferred_element_type=jnp.float32)


def dot_t(a, b):
    return lax.dot_general(a, b, (((1,), (1,)), ((), ())), preferred_element_type=jnp.float32)


def shifted(value, steps):
    count = lax.axis_size("seq")
    initial, last = (max(0, -steps), min(count, count - steps))
    return lax.ppermute(value, "seq", [(source, source + steps) for source in range(initial, last)])


def attention_kernel(scale, lens, here, *refs):
    q_ref, g_ref = refs[0:2]
    far_refs = refs[2 : 2 + REACH]
    k_ref, v_ref = refs[2 + REACH : 4 + REACH]
    outs = refs[-(6 + REACH) :]
    o_ref, dq_ref = outs[0:2]
    part_refs = outs[2 : 2 + REACH]
    own_ref = outs[2 + REACH]
    bias, dkt, dvt = outs[3 + REACH : 6 + REACH]
    rows, width = k_ref.shape
    blocks = REACH + 1
    step = pl.program_id(0)

    @pl.when(step == 0)
    def _():
        base = here[0] * rows
        row = lax.broadcasted_iota(jnp.int32, (rows, width), 0)
        col = lax.broadcasted_iota(jnp.int32, (rows, width), 1)

        def one(i, carry):
            end, start = carry
            end = end + lens[i]
            return end, jnp.where(row >= end - base, end - base, start)

        _, start = lax.fori_loop(
            0, lens.shape[0], one, (jnp.int32(0), jnp.full((rows, width), -base, jnp.int32))
        )
        for t in range(blocks * rows // width):
            pos = col + (t * width - REACH * rows)
            bias[:, t * width : (t + 1) * width] = jnp.where(
                (pos >= start) & (pos <= row), 0.0, NEG
            ).astype(jnp.float32)
        dkt[...] = jnp.zeros_like(dkt)
        dvt[...] = jnp.zeros_like(dvt)

    def key(b):
        return far_refs[b][:, :width] if b < REACH else k_ref[...]

    def val(b):
        return far_refs[b][:, width:] if b < REACH else v_ref[...]

    for h in range(q_ref.shape[1] // width):
        at = slice(h * width, (h + 1) * width)
        q, g = q_ref[:, at], g_ref[:, at]
        s = [dot_t(q, key(b)) + bias[:, b * rows : (b + 1) * rows] for b in range(blocks)]
        top = functools.reduce(jnp.maximum, s).max(axis=1, keepdims=True)
        p = [jnp.exp2((x - top) * (scale * LOG2E)) for x in s]
        total = functools.reduce(jnp.add, p).sum(axis=1, keepdims=True)
        pb = [x.astype(jnp.bfloat16) for x in p]
        o = functools.reduce(jnp.add, [dot(pb[b], val(b)) for b in range(blocks)])
        inverse = 1.0 / total
        o = o * inverse
        o_ref[:, at] = o.astype(jnp.bfloat16)
        gs = (g.astype(jnp.float32) * inverse).astype(jnp.bfloat16)
        delta = jnp.sum(gs.astype(jnp.float32) * o, axis=1, keepdims=True)
        qt, gt = q.T, gs.T
        dq = jnp.zeros((rows, width), jnp.float32)
        for b in range(blocks):
            ds = (p[b] * (dot_t(gs, val(b)) - delta)).astype(jnp.bfloat16)
            dq = dq + dot(ds, key(b))
            dkt[:, b * rows : (b + 1) * rows] += dot(qt, ds)
            dvt[:, b * rows : (b + 1) * rows] += dot(gt, pb[b])
        dq_ref[:, at] = (dq * scale).astype(jnp.bfloat16)

    @pl.when(step == pl.num_programs(0) - 1)
    def _():
        for b in range(blocks):
            at = slice(b * rows, (b + 1) * rows)
            dk = dkt[:, at].T * scale
            dv = dvt[:, at].T
            ref = part_refs[b] if b < REACH else own_ref
            ref[:, :width] = dk.astype(ref.dtype)
            ref[:, width:] = dv.astype(ref.dtype)


def attention(group, lens, here, q, g, keys, values, far, dq_before):
    rows, width = q.shape[0], HEAD_WIDTH
    groups = keys.shape[1] // width
    per_group = q.shape[1] // width // groups
    steps = per_group // HEADS_PER_STEP
    cols = HEADS_PER_STEP * width
    into = pl.BlockSpec((rows, cols), lambda i, *_: (0, group * steps + i))
    out = pl.BlockSpec((rows, cols), lambda i, *_: (0, i))
    own = pl.BlockSpec((rows, width), lambda i, *_: (0, group))
    block = pl.BlockSpec((rows, 2 * width), lambda i, *_: (0, 0))
    extra = [] if dq_before is None else [dq_before]
    alias = {} if dq_before is None else {2 + 2 + REACH + 2: 1}
    flops = 6 * 2 * rows * (REACH + 1) * rows * width * per_group
    return pl.pallas_call(
        functools.partial(attention_kernel, 1.0 / math.sqrt(width)),
        grid_spec=pltpu.PrefetchScalarGridSpec(
            num_scalar_prefetch=2,
            grid=(steps,),
            in_specs=[into, into]
            + [block] * REACH
            + [own, own]
            + [pl.BlockSpec(memory_space=pl.ANY)] * len(extra),
            out_specs=[out, into] + [block] * (REACH + 1),
            scratch_shapes=[
                pltpu.VMEM((rows, (REACH + 1) * rows), jnp.float32),
                pltpu.VMEM((width, (REACH + 1) * rows), jnp.float32),
                pltpu.VMEM((width, (REACH + 1) * rows), jnp.float32),
            ],
        ),
        out_shape=[
            jax.ShapeDtypeStruct((rows, per_group * width), jnp.bfloat16),
            jax.ShapeDtypeStruct(q.shape, jnp.bfloat16),
        ]
        + [jax.ShapeDtypeStruct((rows, 2 * width), jnp.bfloat16)] * REACH
        + [jax.ShapeDtypeStruct((rows, 2 * width), jnp.float32)],
        input_output_aliases=alias,
        compiler_params=pltpu.CompilerParams(vmem_limit_bytes=40 << 20),
        cost_estimate=pl.CostEstimate(flops=flops, bytes_accessed=4 << 20, transcendentals=0),
        name="attention",
    )(lens, here, q, g, *far, keys, values, *extra)


def on_device(queries, keys, values, output_gradient, lengths):
    rows = queries.shape[0]
    width = HEAD_WIDTH
    groups = keys.shape[1] // width
    here = lax.axis_index("seq").reshape(1).astype(jnp.int32)
    fars = []
    for g in range(groups):
        at = slice(g * width, (g + 1) * width)
        pack = jnp.concatenate((keys[:, at], values[:, at]), axis=1)
        fars.append([shifted(pack, dist) for dist in range(REACH, 0, -1)])
    d_queries = None
    heads, sums = [], []
    for g in range(groups):
        out, d_queries, *parts = attention(
            g, lengths, here, queries, output_gradient, keys, values, fars[g], d_queries
        )
        total = parts[REACH]
        for b in range(REACH):
            total = total + shifted(parts[b], b - REACH).astype(jnp.float32)
        sums.append(total)
        split = lax.axis_size("head")
        heads.append(
            lax.all_to_all(
                out.reshape(split, rows // split, out.shape[1]), "head", split_axis=0, concat_axis=0
            )
        )
    both = jnp.stack(heads, axis=2)
    attn_out = jnp.transpose(both, (1, 0, 2, 3)).reshape(both.shape[1], -1)
    key_gradient = jnp.concatenate([s[:, :width] for s in sums], axis=1).astype(jnp.bfloat16)
    value_gradient = jnp.concatenate([s[:, width:] for s in sums], axis=1).astype(jnp.bfloat16)
    return (attn_out, d_queries, key_gradient, value_gradient)


def solution(mesh):
    placed = (P("seq", "head"), P("seq", "head"), P("seq", "head"), P("seq", "head"), P())
    return jax.shard_map(
        on_device,
        mesh=mesh,
        in_specs=placed,
        out_specs=(P(("seq", "head"), None), P("seq", "head"), P("seq", "head"), P("seq", "head")),
        check_vma=False,
    )
```

```python
import functools
import math

import jax
import jax.numpy as jnp
from jax import lax
from jax.experimental import pallas as pl
from jax.experimental.pallas import tpu as pltpu
from jax.sharding import PartitionSpec as P

HEAD_WIDTH = 128
REACH = 4
NEG = -1e30
LOG2E = 1.4426950408889634


def dot(a, b):
    return lax.dot_general(a, b, (((1,), (0,)), ((), ())), preferred_element_type=jnp.float32)


def dot_t(a, b):
    return lax.dot_general(a, b, (((1,), (1,)), ((), ())), preferred_element_type=jnp.float32)


def moved(value, to):
    count = lax.axis_size("seq")
    return lax.ppermute(value, "seq", [(source, to(source) % count) for source in range(count)])


def up(value, steps):
    return moved(value, lambda source: source + steps)


def swapped(value):
    return moved(value, lambda source: source ^ 1)


def mask_kernel(lens, here, bias):
    rows, width = bias.shape[0], HEAD_WIDTH
    base = here[0] * rows
    row = lax.broadcasted_iota(jnp.int32, (rows, width), 0)
    col = lax.broadcasted_iota(jnp.int32, (rows, width), 1)

    def one(i, carry):
        end, start = carry
        end = end + lens[i]
        return end, jnp.where(row >= end - base, end - base, start)

    _, start = lax.fori_loop(
        0, lens.shape[0], one, (jnp.int32(0), jnp.full((rows, width), -base, jnp.int32))
    )
    for t in range(bias.shape[1] // width):
        pos = col + (t * width - REACH * rows)
        bias[:, t * width : (t + 1) * width] = jnp.where(
            (pos >= start) & (pos <= row), 0.0, NEG
        ).astype(jnp.float32)


def mask(lengths, here, rows):
    return pl.pallas_call(
        mask_kernel,
        in_specs=[pl.BlockSpec(memory_space=pltpu.SMEM)] * 2,
        out_specs=pl.BlockSpec(memory_space=pltpu.VMEM),
        out_shape=jax.ShapeDtypeStruct((rows, (REACH + 1) * rows), jnp.float32),
        cost_estimate=pl.CostEstimate(flops=1 << 20, bytes_accessed=1 << 20, transcendentals=0),
        name="mask",
    )(lengths, here)


def attention_kernel(scale, *refs):
    q_ref, g_ref, two_ref, four_ref, odd_ref, k_ref, v_ref, bias_ref = refs[0:8]
    o_ref, dq_ref, two_out, four_out, odd_out, own_out, k_all, v_all = refs[-8:]
    rows, width = k_ref.shape
    far = ((four_ref, 0), (odd_ref, 1), (two_ref, 0), (odd_ref, 0))
    for b, (ref, place) in enumerate(far):
        at = slice(b * rows, (b + 1) * rows)
        k_all[at, :] = ref[:, 2 * place * width : (2 * place + 1) * width]
        v_all[at, :] = ref[:, (2 * place + 1) * width : (2 * place + 2) * width]
    k_all[REACH * rows :, :] = k_ref[...]
    v_all[REACH * rows :, :] = v_ref[...]
    k, v, bias = k_all[...], v_all[...], bias_ref[...]
    dk = dv = None
    for h in range(q_ref.shape[1] // width):
        at = slice(h * width, (h + 1) * width)
        q, g = q_ref[:, at], g_ref[:, at]
        s = dot_t(q, k) + bias
        p = jnp.exp2((s - s.max(axis=1, keepdims=True)) * (scale * LOG2E))
        inverse = 1.0 / p.sum(axis=1, keepdims=True)
        pb = p.astype(jnp.bfloat16)
        o = dot(pb, v) * inverse
        o_ref[:, at] = o.astype(jnp.bfloat16)
        gs = (g.astype(jnp.float32) * inverse).astype(jnp.bfloat16)
        delta = jnp.sum(gs.astype(jnp.float32) * o, axis=1, keepdims=True)
        ds = (p * (dot_t(gs, v) - delta)).astype(jnp.bfloat16)
        dq_ref[:, at] = (dot(ds, k) * scale).astype(jnp.bfloat16)
        dk_part, dv_part = dot(q.T, ds), dot(gs.T, pb)
        dk, dv = (dk_part, dv_part) if dk is None else (dk + dk_part, dv + dv_part)
    parts = ((four_out, 0), (odd_out, 1), (two_out, 0), (odd_out, 0), (own_out, 0))
    for b, (ref, place) in enumerate(parts):
        at = slice(b * rows, (b + 1) * rows)
        for which, grad in enumerate((dk[:, at].T * scale, dv[:, at].T)):
            to = slice((2 * place + which) * width, (2 * place + which + 1) * width)
            ref[:, to] = grad.astype(ref.dtype)


def attention(group, q, g, keys, values, far, bias, before):
    rows, width = q.shape[0], HEAD_WIDTH
    groups = keys.shape[1] // width
    per_group = q.shape[1] // width // groups
    heads = pl.BlockSpec((rows, per_group * width), lambda i: (0, group))
    own = pl.BlockSpec((rows, width), lambda i: (0, group))
    one = pl.BlockSpec((rows, 2 * width), lambda i: (0, 0))
    pair = pl.BlockSpec((rows, 4 * width), lambda i: (0, 0))
    flops = 6 * 2 * rows * (REACH + 1) * rows * width * per_group
    return pl.pallas_call(
        functools.partial(attention_kernel, 1.0 / math.sqrt(width)),
        grid=(1,),
        in_specs=[heads, heads, one, one, pair, own, own, pl.BlockSpec(bias.shape, lambda i: (0, 0))]
        + [pl.BlockSpec(memory_space=pl.ANY)] * len(before),
        out_specs=[heads, heads, one, one, pair, one],
        scratch_shapes=[pltpu.VMEM(((REACH + 1) * rows, width), jnp.bfloat16)] * 2,
        out_shape=[
            jax.ShapeDtypeStruct(q.shape, jnp.bfloat16),
            jax.ShapeDtypeStruct(q.shape, jnp.bfloat16),
            jax.ShapeDtypeStruct((rows, 2 * width), jnp.float32),
            jax.ShapeDtypeStruct((rows, 2 * width), jnp.float32),
            jax.ShapeDtypeStruct((rows, 4 * width), jnp.bfloat16),
            jax.ShapeDtypeStruct((rows, 2 * width), jnp.float32),
        ],
        input_output_aliases={8 + i: i for i in range(len(before))},
        compiler_params=pltpu.CompilerParams(vmem_limit_bytes=40 << 20),
        cost_estimate=pl.CostEstimate(flops=flops, bytes_accessed=4 << 20, transcendentals=0),
        name="attention",
    )(q, g, *far, keys, values, bias, *before)


def on_device(queries, keys, values, output_gradient, lengths):
    rows = queries.shape[0]
    width = HEAD_WIDTH
    groups = keys.shape[1] // width
    place = lax.axis_index("seq")
    even = place % 2 == 0
    packs, twos, fours, fars = [], [], [], []
    for g in range(groups):
        at = slice(g * width, (g + 1) * width)
        packs.append(jnp.concatenate((keys[:, at], values[:, at]), axis=1))
    for pack in packs:
        twos.append(up(pack, 2))
        fours.append(up(pack, 4))
    bias = mask(lengths, place.reshape(1).astype(jnp.int32), rows)
    for pack, two, four in zip(packs, twos, fours):
        near = jnp.where(even, pack, two)
        far = jnp.where(even, two, four)
        fars.append((two, four, swapped(jnp.concatenate((near, far), axis=1))))
    before = ()
    sums = []
    for g in range(groups):
        out, d_queries, two, four, odd, own = attention(
            g, queries, output_gradient, keys, values, fars[g], bias, before
        )
        before = (out, d_queries)
        other = swapped(odd).astype(jnp.float32)
        one, three = other[:, : 2 * width], other[:, 2 * width :]
        two = (two + jnp.where(even, three, one)).astype(jnp.bfloat16)
        four = (four + jnp.where(even, 0.0, three)).astype(jnp.bfloat16)
        own = own + jnp.where(even, one, 0.0)
        sums.append(own + up(two, -2).astype(jnp.float32) + up(four, -4).astype(jnp.float32))
    split = lax.axis_size("head")
    got = lax.all_to_all(
        out.reshape(split, rows // split, out.shape[1]), "head", split_axis=0, concat_axis=0
    )
    attn_out = jnp.transpose(got, (1, 0, 2)).reshape(got.shape[1], -1)
    key_gradient = jnp.concatenate([s[:, :width] for s in sums], axis=1).astype(jnp.bfloat16)
    value_gradient = jnp.concatenate([s[:, width:] for s in sums], axis=1).astype(jnp.bfloat16)
    return (attn_out, d_queries, key_gradient, value_gradient)


def solution(mesh):
    placed = (P("seq", "head"), P("seq", "head"), P("seq", "head"), P("seq", "head"), P())
    return jax.shard_map(
        on_device,
        mesh=mesh,
        in_specs=placed,
        out_specs=(P(("seq", "head"), None), P("seq", "head"), P("seq", "head"), P("seq", "head")),
        check_vma=False,
    )
```

```python
import functools
import math

import jax
import jax.numpy as jnp
from jax import lax
from jax.experimental import pallas as pl
from jax.experimental.pallas import tpu as pltpu
from jax.sharding import PartitionSpec as P

HEAD_WIDTH = 128
REACH = 4
NEG = -1e30
LOG2E = 1.4426950408889634


def dot(a, b):
    return lax.dot_general(a, b, (((1,), (0,)), ((), ())), preferred_element_type=jnp.float32)


def dot_t(a, b):
    return lax.dot_general(a, b, (((1,), (1,)), ((), ())), preferred_element_type=jnp.float32)


def moved(value, to):
    count = lax.axis_size("seq")
    return lax.ppermute(value, "seq", [(source, to(source) % count) for source in range(count)])


def up(value, steps):
    return moved(value, lambda source: source + steps)


def swapped(value):
    return moved(value, lambda source: source ^ 1)


def own_forward_kernel(scale, lens, here, q_ref, k_ref, v_ref, out_ref, stat_ref, near_ref, far_ref):
    rows, width = k_ref.shape[0], HEAD_WIDTH
    base = here[0] * rows
    row = lax.broadcasted_iota(jnp.int32, (rows, width), 0)
    col = lax.broadcasted_iota(jnp.int32, (rows, width), 1)

    def one(i, carry):
        end, start = carry
        end = end + lens[i]
        return end, jnp.where(row >= end - base, end - base, start)

    _, start = lax.fori_loop(
        0, lens.shape[0], one, (jnp.int32(0), jnp.full((rows, width), -base, jnp.int32))
    )
    for t in range(REACH * rows // width):
        pos = col + (t * width - REACH * rows)
        far_ref[:, t * width : (t + 1) * width] = jnp.where(pos >= start, 0.0, NEG).astype(jnp.float32)
    for t in range(rows // width):
        pos = col + t * width
        near_ref[:, t * width : (t + 1) * width] = jnp.where(
            (pos >= start) & (pos <= row), 0.0, NEG
        ).astype(jnp.float32)
    near = near_ref[...]
    heads = q_ref.shape[1] // width
    group = heads // (k_ref.shape[1] // width)
    for h in range(heads):
        at = slice(h * width, (h + 1) * width)
        kv = slice(h // group * width, (h // group + 1) * width)
        s = dot_t(q_ref[:, at], k_ref[:, kv]) + near
        top = s.max(axis=1, keepdims=True)
        p = jnp.exp2((s - top) * (scale * LOG2E))
        stat_ref[:, h : h + 1] = top
        stat_ref[:, heads + h : heads + h + 1] = p.sum(axis=1, keepdims=True)
        out_ref[:, at] = dot(p.astype(jnp.bfloat16), v_ref[:, kv])


def far_kernel(scale, *refs):
    q_ref, g_ref, out_ref, stat_ref, bias_ref = refs[0:5]
    o_ref, dq_out, keep_ref, two_out, four_out, odd_out, k_all, v_all, dq_ref, sent = refs[-10:]
    fars = refs[5:-10]
    rows, width = q_ref.shape[0], HEAD_WIDTH
    heads = q_ref.shape[1] // width
    groups = len(fars) // 3
    factor = scale * LOG2E
    bias = bias_ref[...]
    for n in range(groups):
        two_ref, four_ref, odd_ref = fars[3 * n : 3 * n + 3]
        for b, (ref, place) in enumerate(((four_ref, 0), (odd_ref, 1), (two_ref, 0), (odd_ref, 0))):
            at = slice(b * rows, (b + 1) * rows)
            k_all[n, at, :] = ref[:, 2 * place * width : (2 * place + 1) * width]
            v_all[n, at, :] = ref[:, (2 * place + 1) * width : (2 * place + 2) * width]
        k, v = k_all[n], v_all[n]
        dk = dv = None
        for h in range(n * heads // groups, (n + 1) * heads // groups):
            at = slice(h * width, (h + 1) * width)
            q, g = q_ref[:, at], g_ref[:, at]
            top = stat_ref[:, h : h + 1]
            total = stat_ref[:, heads + h : heads + h + 1]
            s = dot_t(q, k) + bias
            most = jnp.maximum(top, s.max(axis=1, keepdims=True))
            p = jnp.exp2((s - most) * factor)
            keep = jnp.exp2((top - most) * factor)
            total = total * keep + p.sum(axis=1, keepdims=True)
            inverse = 1.0 / total
            pb = p.astype(jnp.bfloat16)
            o = (dot(pb, v) + out_ref[:, at] * keep) * inverse
            o_ref[:, at] = o.astype(jnp.bfloat16)
            gs = (g.astype(jnp.float32) * inverse).astype(jnp.bfloat16)
            delta = jnp.sum(gs.astype(jnp.float32) * o, axis=1, keepdims=True)
            keep_ref[:, h : h + 1] = most
            keep_ref[:, heads + h : heads + h + 1] = inverse
            keep_ref[:, 2 * heads + h : 2 * heads + h + 1] = delta
            ds = (p * (dot_t(gs, v) - delta)).astype(jnp.bfloat16)
            dq_ref[:, at] = dot(ds, k)
            pltpu.make_async_copy(dq_ref.at[:, at], dq_out.at[:, at], sent.at[h]).start()
            dk_part, dv_part = dot(q.T, ds), dot(gs.T, pb)
            dk, dv = (dk_part, dv_part) if dk is None else (dk + dk_part, dv + dv_part)
        for b, (ref, place) in enumerate(((four_out, 0), (odd_out, 1), (two_out, 0), (odd_out, 0))):
            at = slice(b * rows, (b + 1) * rows)
            for which, grad in enumerate((dk[:, at].T * scale, dv[:, at].T)):
                to = (2 * groups * place + 2 * n + which) * width
                ref[:, to : to + width] = grad.astype(ref.dtype)
    for h in range(heads):
        at = slice(h * width, (h + 1) * width)
        pltpu.make_async_copy(dq_ref.at[:, at], dq_out.at[:, at], sent.at[h]).wait()


def own_backward_kernel(scale, q_ref, g_ref, k_ref, v_ref, bias_ref, keep_ref, far_ref, dq_ref, own_ref):
    rows, width = q_ref.shape[0], HEAD_WIDTH
    heads = q_ref.shape[1] // width
    groups = k_ref.shape[1] // width
    bias = bias_ref[...]
    for n in range(groups):
        k, v = k_ref[:, n * width : (n + 1) * width], v_ref[:, n * width : (n + 1) * width]
        dk = dv = None
        for h in range(n * heads // groups, (n + 1) * heads // groups):
            at = slice(h * width, (h + 1) * width)
            q = q_ref[:, at]
            most = keep_ref[:, h : h + 1]
            inverse = keep_ref[:, heads + h : heads + h + 1]
            delta = keep_ref[:, 2 * heads + h : 2 * heads + h + 1]
            gs = (g_ref[:, at].astype(jnp.float32) * inverse).astype(jnp.bfloat16)
            p = jnp.exp2((dot_t(q, k) + bias - most) * (scale * LOG2E))
            ds = (p * (dot_t(gs, v) - delta)).astype(jnp.bfloat16)
            dq_ref[:, at] = ((far_ref[:, at] + dot(ds, k)) * scale).astype(jnp.bfloat16)
            dk_part, dv_part = dot(q.T, ds), dot(gs.T, p.astype(jnp.bfloat16))
            dk, dv = (dk_part, dv_part) if dk is None else (dk + dk_part, dv + dv_part)
        own_ref[:, 2 * n * width : (2 * n + 1) * width] = dk.T * scale
        own_ref[:, (2 * n + 1) * width : (2 * n + 2) * width] = dv.T


def choose_kernel(scale, place, own_ref, two_ref, four_ref, send_ref):
    even = place[0] % 2 == 0
    half = own_ref.shape[1]

    @pl.when(even)
    def _():
        send_ref[:, :half] = own_ref[...]
        send_ref[:, half:] = two_ref[...]

    @pl.when(jnp.logical_not(even))
    def _():
        send_ref[:, :half] = two_ref[...]
        send_ref[:, half:] = four_ref[...]


def join_kernel(scale, place, two_ref, four_ref, other_ref, two_out, four_out):
    even = place[0] % 2 == 0
    half = two_ref.shape[1]

    @pl.when(even)
    def _():
        three = other_ref[:, half:].astype(jnp.float32)
        two_out[...] = (two_ref[...] + three).astype(jnp.bfloat16)
        four_out[...] = four_ref[...].astype(jnp.bfloat16)

    @pl.when(jnp.logical_not(even))
    def _():
        one = other_ref[:, :half].astype(jnp.float32)
        three = other_ref[:, half:].astype(jnp.float32)
        two_out[...] = (two_ref[...] + one).astype(jnp.bfloat16)
        four_out[...] = (four_ref[...] + three).astype(jnp.bfloat16)


def total_kernel(scale, place, own_ref, other_ref, two_ref, four_ref, k_out, v_out):
    width = HEAD_WIDTH
    one = jnp.where(place[0] % 2 == 0, 1.0, 0.0)
    for n in range(k_out.shape[1] // width):
        for which, ref in enumerate((k_out, v_out)):
            at = slice((2 * n + which) * width, (2 * n + which + 1) * width)
            total = own_ref[:, at] + other_ref[:, at].astype(jnp.float32) * one
            total = total + two_ref[:, at].astype(jnp.float32) + four_ref[:, at].astype(jnp.float32)
            ref[:, n * width : (n + 1) * width] = total.astype(jnp.bfloat16)


def call(kernel, name, matmuls, outs, *args, scalars=0, scratch=(), hbm=()):
    whole = pl.BlockSpec(memory_space=pltpu.VMEM)
    return pl.pallas_call(
        functools.partial(kernel, 1.0 / math.sqrt(HEAD_WIDTH)),
        in_specs=[pl.BlockSpec(memory_space=pltpu.SMEM)] * scalars + [whole] * (len(args) - scalars),
        out_specs=[pl.BlockSpec(memory_space=pl.ANY) if i in hbm else whole for i in range(len(outs))],
        out_shape=[jax.ShapeDtypeStruct(shape, dtype) for shape, dtype in outs],
        scratch_shapes=scratch,
        compiler_params=pltpu.CompilerParams(vmem_limit_bytes=16 << 20),
        cost_estimate=pl.CostEstimate(
            flops=matmuls * 2 * 256 * 256 * 128 * 16, bytes_accessed=4 << 20, transcendentals=0
        ),
        name=name,
    )(*args)


def on_device(queries, keys, values, output_gradient, lengths):
    rows, width = queries.shape[0], HEAD_WIDTH
    groups = keys.shape[1] // width
    heads = queries.shape[1] // width
    place = lax.axis_index("seq")
    here = place.reshape(1).astype(jnp.int32)
    packs, twos, fours, fars = [], [], [], []
    for g in range(groups):
        at = slice(g * width, (g + 1) * width)
        packs.append(jnp.concatenate((keys[:, at], values[:, at]), axis=1))
    for pack in packs:
        twos.append(up(pack, 2))
        fours.append(up(pack, 4))
    parts, stats, near_bias, far_bias = call(
        own_forward_kernel,
        "own_forward",
        2,
        [
            (queries.shape, jnp.float32),
            ((rows, 2 * heads), jnp.float32),
            ((rows, rows), jnp.float32),
            ((rows, REACH * rows), jnp.float32),
        ],
        lengths,
        here,
        queries,
        keys,
        values,
        scalars=2,
    )
    packs, stats = lax.optimization_barrier((packs, stats))
    for pack, two, four in zip(packs, twos, fours):
        send = call(
            choose_kernel,
            "choose",
            0,
            [((rows, 4 * width), jnp.bfloat16)],
            here,
            pack,
            two,
            four,
            scalars=1,
        )[0]
        fars += [two, four, swapped(send)]
    wide = 2 * groups * width
    out, dq_far, keep, two, four, odd = call(
        far_kernel,
        "far",
        6 * REACH,
        [
            (queries.shape, jnp.bfloat16),
            (queries.shape, jnp.float32),
            ((rows, 3 * heads), jnp.float32),
            ((rows, wide), jnp.float32),
            ((rows, wide), jnp.float32),
            ((rows, 2 * wide), jnp.bfloat16),
        ],
        queries,
        output_gradient,
        parts,
        stats,
        far_bias,
        *fars,
        scratch=[pltpu.VMEM((groups, REACH * rows, width), jnp.bfloat16)] * 2
        + [pltpu.VMEM(queries.shape, jnp.float32), pltpu.SemaphoreType.DMA((heads,))],
        hbm=(1,),
    )
    other = swapped(odd)
    two, four = call(
        join_kernel,
        "join",
        0,
        [((rows, wide), jnp.bfloat16)] * 2,
        here,
        two,
        four,
        other,
        scalars=1,
    )
    two, four = up(two, -2), up(four, -4)
    split = lax.axis_size("head")
    got = lax.all_to_all(
        out.reshape(split, rows // split, out.shape[1]), "head", split_axis=0, concat_axis=0
    )
    d_queries, own = call(
        own_backward_kernel,
        "own_backward",
        5,
        [(queries.shape, jnp.bfloat16), ((rows, wide), jnp.float32)],
        queries,
        output_gradient,
        keys,
        values,
        near_bias,
        keep,
        dq_far,
    )
    key_gradient, value_gradient = call(
        total_kernel,
        "total",
        0,
        [(keys.shape, jnp.bfloat16)] * 2,
        here,
        own,
        other,
        two,
        four,
        scalars=1,
    )
    attn_out = jnp.transpose(got, (1, 0, 2)).reshape(got.shape[1], -1)
    return (attn_out, d_queries, key_gradient, value_gradient)


def solution(mesh):
    placed = (P("seq", "head"), P("seq", "head"), P("seq", "head"), P("seq", "head"), P())
    return jax.shard_map(
        on_device,
        mesh=mesh,
        in_specs=placed,
        out_specs=(P(("seq", "head"), None), P("seq", "head"), P("seq", "head"), P("seq", "head")),
        check_vma=False,
    )
```

```python
import functools
import math

import jax
import jax.numpy as jnp
from jax import lax
from jax.experimental import pallas as pl
from jax.experimental.pallas import tpu as pltpu
from jax.sharding import PartitionSpec as P

HEAD_WIDTH = 128
REACH = 4
NEG = -1e30
LOG2E = 1.4426950408889634


def dot(a, b):
    return lax.dot_general(a, b, (((1,), (0,)), ((), ())), preferred_element_type=jnp.float32)


def dot_t(a, b):
    return lax.dot_general(a, b, (((1,), (1,)), ((), ())), preferred_element_type=jnp.float32)


def moved(value, to):
    count = lax.axis_size("seq")
    return lax.ppermute(value, "seq", [(source, to(source) % count) for source in range(count)])


def up(value, steps):
    return moved(value, lambda source: source + steps)


def swapped(value):
    return moved(value, lambda source: source ^ 1)


def first_seen(lens, here, rows, width):
    base = here[0] * rows
    row = lax.broadcasted_iota(jnp.int32, (rows, width), 0)

    def one(i, carry):
        end, start = carry
        end = end + lens[i]
        return end, jnp.where(row >= end - base, end - base, start)

    first = (jnp.int32(0), jnp.full((rows, width), -base, jnp.int32))
    return lax.fori_loop(0, lens.shape[0], one, first)[1]


def mask(start, distance):
    row = lax.broadcasted_iota(jnp.int32, start.shape, 0)
    pos = lax.broadcasted_iota(jnp.int32, start.shape, 1) - distance
    seen = pos >= start if distance >= start.shape[0] else (pos >= start) & (pos <= row)
    return jnp.where(seen, 0.0, NEG).astype(jnp.float32)


def near_mask(start, rows):
    width = start.shape[1]
    return jnp.concatenate([mask(start, -at) for at in range(0, rows, width)], axis=1)


def own_forward_kernel(scale, lens, here, q_ref, *refs):
    out_ref, top_ref, sum_ref, far_ref = refs[-4:]
    rows, width = q_ref.shape[0], HEAD_WIDTH
    start = first_seen(lens, here, rows, width)
    for at in range(0, REACH * rows, width):
        far_ref[:, at : at + width] = mask(start, REACH * rows - at)
    near = near_mask(start, rows)
    groups = len(refs) - 4
    heads = q_ref.shape[1] // width
    for h in range(heads):
        at = slice(h * width, (h + 1) * width)
        pack = refs[h * groups // heads]
        s = dot_t(q_ref[:, at], pack[:, :width]) + near
        top = s.max(axis=1, keepdims=True)
        p = jnp.exp2((s - top) * (scale * LOG2E))
        top_ref[:, at] = jnp.broadcast_to(top, (rows, width))
        sum_ref[:, at] = jnp.broadcast_to(p.sum(axis=1, keepdims=True), (rows, width))
        out_ref[:, at] = dot(p.astype(jnp.bfloat16), pack[:, width:])


def far_kernel(scale, *refs):
    q_ref, g_ref, out_ref, top_ref, sum_ref, bias_ref = refs[0:6]
    (o_out, dq_out, keep_out, two_out, four_out, odd_out) = refs[-12:-6]
    k_all, v_all, o_ref, dq_ref, keep_ref, sent = refs[-6:]
    fars = refs[6:-12]
    rows, width = q_ref.shape[0], HEAD_WIDTH
    groups = len(fars) // 3
    heads = q_ref.shape[1] // width
    share = heads // groups
    factor = scale * LOG2E
    bias = bias_ref[...]
    for n in range(groups):
        two_ref, four_ref, odd_ref = fars[3 * n : 3 * n + 3]
        for b, (ref, place) in enumerate(((four_ref, 0), (odd_ref, 1), (two_ref, 0), (odd_ref, 0))):
            at = slice(b * rows, (b + 1) * rows)
            k_all[n, at, :] = ref[:, 2 * place * width : (2 * place + 1) * width]
            v_all[n, at, :] = ref[:, (2 * place + 1) * width : (2 * place + 2) * width]

    def weigh(h):
        at = slice(h * width, (h + 1) * width)
        q, top = q_ref[:, at], top_ref[:, at]
        s = dot_t(q, k_all[h // share]) + bias
        most = jnp.maximum(top, s.max(axis=1, keepdims=True))
        p = jnp.exp2((s - jnp.tile(most, (1, s.shape[1] // width))) * factor)
        keep = jnp.exp2((top - most) * factor)
        total = sum_ref[:, at] * keep + p.sum(axis=1, keepdims=True)
        return at, q, p, most, keep, total

    def send(n):
        to = slice(n * share * width, (n + 1) * share * width)
        pairs = [(o_ref.at[:, to], o_out.at[:, to]), (dq_ref.at[:, to], dq_out.at[:, to])]
        if n == groups - 1:
            pairs.append((keep_ref, keep_out))
        return [pltpu.make_async_copy(*pair, sent.at[2 * n + i]) for i, pair in enumerate(pairs)]

    ahead = weigh(0)
    for h in range(heads):
        n = h // share
        at, q, p, most, keep, total = ahead
        ahead = weigh(h + 1) if h + 1 < heads else None
        k, v = k_all[n], v_all[n]
        inverse = 1.0 / total
        pb = p.astype(jnp.bfloat16)
        o = (dot(pb, v) + out_ref[:, at] * keep) * inverse
        o_ref[:, at] = o.astype(jnp.bfloat16)
        gs = (g_ref[:, at].astype(jnp.float32) * inverse).astype(jnp.bfloat16)
        delta = jnp.sum(gs.astype(jnp.float32) * o, axis=1, keepdims=True)
        keep_ref[:, h : h + 1] = most[:, :1] * factor + jnp.log2(total[:, :1])
        keep_ref[:, heads + h : heads + h + 1] = delta * total[:, :1]
        ds = (p * (dot_t(gs, v) - delta)).astype(jnp.bfloat16)
        dq_ref[:, at] = dot(ds, k).astype(jnp.bfloat16)
        dk_part, dv_part = dot(q.T, ds), dot(gs.T, pb)
        dk, dv = (dk_part, dv_part) if h % share == 0 else (dk + dk_part, dv + dv_part)
        if h % share == share - 1:
            for copy in send(n):
                copy.start()
            outs = ((four_out, 0), (odd_out, 1), (two_out, 0), (odd_out, 0))
            for b, (ref, place) in enumerate(outs):
                at = slice(b * rows, (b + 1) * rows)
                for which, grad in enumerate((dk[:, at].T * scale, dv[:, at].T)):
                    to = (2 * groups * place + 2 * n + which) * width
                    ref[:, to : to + width] = grad.astype(ref.dtype)
    for n in range(groups):
        for copy in send(n):
            copy.wait()


def own_backward_kernel(scale, lens, here, q_ref, g_ref, far_ref, keep_ref, *refs):
    dq_ref, own_ref = refs[-2:]
    rows, width = q_ref.shape[0], HEAD_WIDTH
    groups = len(refs) - 2
    heads = q_ref.shape[1] // width
    share = heads // groups
    factor = scale * LOG2E
    bias = near_mask(first_seen(lens, here, rows, width), rows)
    for h in range(heads):
        n = h // share
        k, v = refs[n][:, :width], refs[n][:, width:]
        at = slice(h * width, (h + 1) * width)
        q, g = q_ref[:, at], g_ref[:, at]
        p = jnp.exp2((dot_t(q, k) + bias) * factor - keep_ref[:, h : h + 1])
        ds = (p * (dot_t(g, v) - keep_ref[:, heads + h : heads + h + 1])).astype(jnp.bfloat16)
        dq = far_ref[:, at].astype(jnp.float32) + dot(ds, k)
        dq_ref[:, at] = (dq * scale).astype(jnp.bfloat16)
        dk_part, dv_part = dot(q.T, ds), dot(g.T, p.astype(jnp.bfloat16))
        dk, dv = (dk_part, dv_part) if h % share == 0 else (dk + dk_part, dv + dv_part)
        if h % share == share - 1:
            own_ref[:, 2 * n * width : (2 * n + 1) * width] = dk.T * scale
            own_ref[:, (2 * n + 1) * width : (2 * n + 2) * width] = dv.T


def choose_kernel(scale, place, own_ref, two_ref, four_ref, send_ref):
    even = place[0] % 2 == 0
    half = own_ref.shape[1]

    @pl.when(even)
    def _():
        send_ref[:, :half] = own_ref[...]
        send_ref[:, half:] = two_ref[...]

    @pl.when(jnp.logical_not(even))
    def _():
        send_ref[:, :half] = two_ref[...]
        send_ref[:, half:] = four_ref[...]


def join_kernel(scale, place, two_ref, four_ref, other_ref, two_out, four_out):
    even = place[0] % 2 == 0
    half = two_ref.shape[1]

    @pl.when(even)
    def _():
        three = other_ref[:, half:].astype(jnp.float32)
        two_out[...] = (two_ref[...] + three).astype(jnp.bfloat16)
        four_out[...] = four_ref[...].astype(jnp.bfloat16)

    @pl.when(jnp.logical_not(even))
    def _():
        one = other_ref[:, :half].astype(jnp.float32)
        three = other_ref[:, half:].astype(jnp.float32)
        two_out[...] = (two_ref[...] + one).astype(jnp.bfloat16)
        four_out[...] = (four_ref[...] + three).astype(jnp.bfloat16)


def total_kernel(scale, place, own_ref, other_ref, two_ref, four_ref, k_out, v_out):
    width = HEAD_WIDTH
    one = jnp.where(place[0] % 2 == 0, 1.0, 0.0)
    for n in range(k_out.shape[1] // width):
        for which, ref in enumerate((k_out, v_out)):
            at = slice((2 * n + which) * width, (2 * n + which + 1) * width)
            total = own_ref[:, at] + other_ref[:, at].astype(jnp.float32) * one
            total = total + two_ref[:, at].astype(jnp.float32) + four_ref[:, at].astype(jnp.float32)
            ref[:, n * width : (n + 1) * width] = total.astype(jnp.bfloat16)


def call(kernel, name, cost, outs, *args, scalars=0, scratch=(), hbm=()):
    whole = pl.BlockSpec(memory_space=pltpu.VMEM)
    left = pl.BlockSpec(memory_space=pltpu.HBM)
    return pl.pallas_call(
        functools.partial(kernel, 1.0 / math.sqrt(HEAD_WIDTH)),
        in_specs=[pl.BlockSpec(memory_space=pltpu.SMEM)] * scalars + [whole] * (len(args) - scalars),
        out_specs=[left if i in hbm else whole for i in range(len(outs))],
        out_shape=[jax.ShapeDtypeStruct(shape, dtype) for shape, dtype in outs],
        scratch_shapes=scratch,
        compiler_params=pltpu.CompilerParams(vmem_limit_bytes=20 << 20),
        cost_estimate=pl.CostEstimate(
            flops=cost << 20, bytes_accessed=1 << 20, transcendentals=0
        ),
        name=name,
    )(*args)


def on_device(queries, keys, values, output_gradient, lengths):
    rows, width = queries.shape[0], HEAD_WIDTH
    groups = keys.shape[1] // width
    heads = queries.shape[1] // width
    wide = 2 * groups * width
    place = lax.axis_index("seq")
    here = place.reshape(1).astype(jnp.int32)
    packs, twos, fours, fars = [], [], [], []
    for n in range(groups):
        at = slice(n * width, (n + 1) * width)
        packs.append(jnp.concatenate((keys[:, at], values[:, at]), axis=1))
    for pack in packs:
        twos.append(up(pack, 2))
        fours.append(up(pack, 4))
    parts, top, total, bias = call(
        own_forward_kernel,
        "own_forward",
        512,
        [(queries.shape, jnp.float32)] * 3 + [((rows, REACH * rows), jnp.float32)],
        lengths,
        here,
        queries,
        *packs,
        scalars=2,
    )
    packs, bias = lax.optimization_barrier((packs, bias))
    for pack, two, four in zip(packs, twos, fours):
        send = call(
            choose_kernel,
            "choose",
            0,
            [((rows, 4 * width), jnp.bfloat16)],
            here,
            pack,
            two,
            four,
            scalars=1,
        )[0]
        fars += [two, four, swapped(send)]
    out, dq_far, keep, two, four, odd = call(
        far_kernel,
        "far",
        6 * 1024,
        [
            (queries.shape, jnp.bfloat16),
            (queries.shape, jnp.bfloat16),
            ((rows, width), jnp.float32),
            ((rows, wide), jnp.float32),
            ((rows, wide), jnp.float32),
            ((rows, 2 * wide), jnp.bfloat16),
        ],
        queries,
        output_gradient,
        parts,
        top,
        total,
        bias,
        *fars,
        scratch=[pltpu.VMEM((groups, REACH * rows, width), jnp.bfloat16)] * 2
        + [pltpu.VMEM(queries.shape, jnp.bfloat16)] * 2
        + [pltpu.VMEM((rows, width), jnp.float32), pltpu.SemaphoreType.DMA((2 * groups + 1,))],
        hbm=(0, 1, 2),
    )
    other = swapped(odd)
    two, four = call(
        join_kernel,
        "join",
        0,
        [((rows, wide), jnp.bfloat16)] * 2,
        here,
        two,
        four,
        other,
        scalars=1,
    )
    two_back, four_back = up(two, -2), up(four, -4)
    split = lax.axis_size("head")
    got = lax.all_to_all(
        out.reshape(split, rows // split, out.shape[1]), "head", split_axis=0, concat_axis=0
    )
    keep, two = lax.optimization_barrier((keep, two))
    d_queries, own = call(
        own_backward_kernel,
        "own_backward",
        1024,
        [(queries.shape, jnp.bfloat16), ((rows, wide), jnp.float32)],
        lengths,
        here,
        queries,
        output_gradient,
        dq_far,
        keep,
        *packs,
        scalars=2,
    )
    key_gradient, value_gradient = call(
        total_kernel,
        "total",
        0,
        [(keys.shape, jnp.bfloat16)] * 2,
        here,
        own,
        other,
        two_back,
        four_back,
        scalars=1,
    )
    attn_out = jnp.transpose(got, (1, 0, 2)).reshape(got.shape[1], -1)
    return (attn_out, d_queries, key_gradient, value_gradient)


def solution(mesh):
    placed = (P("seq", "head"), P("seq", "head"), P("seq", "head"), P("seq", "head"), P())
    return jax.shard_map(
        on_device,
        mesh=mesh,
        in_specs=placed,
        out_specs=(P(("seq", "head"), None), P("seq", "head"), P("seq", "head"), P("seq", "head")),
        check_vma=False,
    )
```

```python
import functools
import math

import jax
import jax.numpy as jnp
from jax import lax
from jax.experimental import pallas as pl
from jax.experimental.pallas import tpu as pltpu
from jax.sharding import PartitionSpec as P

HEAD_WIDTH = 128
REACH = 4
NEG = -1e30
LOG2E = 1.4426950408889634


def dot(a, b):
    return lax.dot_general(a, b, (((1,), (0,)), ((), ())), preferred_element_type=jnp.float32)


def dot_t(a, b):
    return lax.dot_general(a, b, (((1,), (1,)), ((), ())), preferred_element_type=jnp.float32)


def moved(value, to):
    count = lax.axis_size("seq")
    return lax.ppermute(value, "seq", [(source, to(source) % count) for source in range(count)])


def up(value, steps):
    return moved(value, lambda source: source + steps)


def swapped(value):
    return moved(value, lambda source: source ^ 1)


def first_seen(lens, here, rows, width):
    base = here[0] * rows
    row = lax.broadcasted_iota(jnp.int32, (rows, width), 0)

    def one(i, carry):
        end, start = carry
        end = end + lens[i]
        return end, jnp.where(row >= end - base, end - base, start)

    first = (jnp.int32(0), jnp.full((rows, width), -base, jnp.int32))
    return lax.fori_loop(0, lens.shape[0], one, first)[1]


def mask(start, distance):
    row = lax.broadcasted_iota(jnp.int32, start.shape, 0)
    pos = lax.broadcasted_iota(jnp.int32, start.shape, 1) - distance
    seen = pos >= start if distance >= start.shape[0] else (pos >= start) & (pos <= row)
    return jnp.where(seen, 0.0, NEG).astype(jnp.float32)


def near_mask(start, rows):
    width = start.shape[1]
    return jnp.concatenate([mask(start, -at) for at in range(0, rows, width)], axis=1)


def own_forward_kernel(
    scale, lens, here, q_ref, k_ref, v_ref, out_ref, top_ref, sum_ref, far_ref
):
    rows, width = q_ref.shape[0], HEAD_WIDTH
    start = first_seen(lens, here, rows, width)
    for at in range(0, REACH * rows, width):
        far_ref[:, at : at + width] = mask(start, REACH * rows - at)
    near = near_mask(start, rows)
    heads = q_ref.shape[1] // width
    share = q_ref.shape[1] // k_ref.shape[1]
    for h in range(heads):
        at = slice(h * width, (h + 1) * width)
        kv = slice(h // share * width, (h // share + 1) * width)
        s = dot_t(q_ref[:, at], k_ref[:, kv]) + near
        top = s.max(axis=1, keepdims=True)
        p = jnp.exp2((s - top) * (scale * LOG2E))
        top_ref[:, at] = jnp.broadcast_to(top, (rows, width))
        sum_ref[:, at] = jnp.broadcast_to(p.sum(axis=1, keepdims=True), (rows, width))
        out_ref[:, at] = dot(p.astype(jnp.bfloat16), v_ref[:, kv])


def far_kernel(scale, *refs):
    q_ref, g_ref, out_ref, top_ref, sum_ref, bias_ref = refs[0:6]
    (o_out, dq_out, keep_out, two_out, four_out, odd_out) = refs[-12:-6]
    k_all, v_all, o_ref, dq_ref, keep_ref, sent = refs[-6:]
    fars = refs[6:-12]
    rows, width = q_ref.shape[0], HEAD_WIDTH
    groups = k_all.shape[0]
    heads = q_ref.shape[1] // width
    share = heads // groups
    factor = scale * LOG2E
    bias = bias_ref[...]
    for which, to in enumerate((k_all, v_all)):
        two_ref, four_ref, odd_ref = fars[3 * which : 3 * which + 3]
        for b, (ref, place) in enumerate(((four_ref, 0), (odd_ref, 1), (two_ref, 0), (odd_ref, 0))):
            for n in range(groups):
                column = (groups * place + n) * width
                to[n, b * rows : (b + 1) * rows, :] = ref[:, column : column + width]

    def weigh(h):
        at = slice(h * width, (h + 1) * width)
        q, top = q_ref[:, at], top_ref[:, at]
        s = dot_t(q, k_all[h // share]) + bias
        most = jnp.maximum(top, s.max(axis=1, keepdims=True))
        p = jnp.exp2((s - jnp.tile(most, (1, s.shape[1] // width))) * factor)
        keep = jnp.exp2((top - most) * factor)
        total = sum_ref[:, at] * keep + p.sum(axis=1, keepdims=True)
        return at, q, p, most, keep, total

    def send(n):
        to = slice(n * share * width, (n + 1) * share * width)
        pairs = [(o_ref.at[:, to], o_out.at[:, to]), (dq_ref.at[:, to], dq_out.at[:, to])]
        if n == groups - 1:
            pairs.append((keep_ref, keep_out))
        return [pltpu.make_async_copy(*pair, sent.at[2 * n + i]) for i, pair in enumerate(pairs)]

    ahead = weigh(0)
    for h in range(heads):
        n = h // share
        at, q, p, most, keep, total = ahead
        ahead = weigh(h + 1) if h + 1 < heads else None
        k, v = k_all[n], v_all[n]
        inverse = 1.0 / total
        pb = p.astype(jnp.bfloat16)
        o = (dot(pb, v) + out_ref[:, at] * keep) * inverse
        o_ref[:, at] = o.astype(jnp.bfloat16)
        gs = (g_ref[:, at].astype(jnp.float32) * inverse).astype(jnp.bfloat16)
        delta = jnp.sum(gs.astype(jnp.float32) * o, axis=1, keepdims=True)
        keep_ref[:, h : h + 1] = most[:, :1] * factor + jnp.log2(total[:, :1])
        keep_ref[:, heads + h : heads + h + 1] = delta * total[:, :1]
        ds = (p * (dot_t(gs, v) - delta)).astype(jnp.bfloat16)
        dq_ref[:, at] = dot(ds, k).astype(jnp.bfloat16)
        dk_part, dv_part = dot(q.T, ds), dot(gs.T, pb)
        dk, dv = (dk_part, dv_part) if h % share == 0 else (dk + dk_part, dv + dv_part)
        if h % share == share - 1:
            for copy in send(n):
                copy.start()
            outs = ((four_out, 0), (odd_out, 1), (two_out, 0), (odd_out, 0))
            for b, (ref, place) in enumerate(outs):
                at = slice(b * rows, (b + 1) * rows)
                for which, grad in enumerate((dk[:, at].T * scale, dv[:, at].T)):
                    to = (2 * groups * place + 2 * n + which) * width
                    ref[:, to : to + width] = grad.astype(ref.dtype)
    for n in range(groups):
        for copy in send(n):
            copy.wait()


def own_backward_kernel(
    scale, lens, here, q_ref, g_ref, far_ref, keep_ref, k_ref, v_ref, dq_ref, own_ref
):
    rows, width = q_ref.shape[0], HEAD_WIDTH
    heads = q_ref.shape[1] // width
    share = q_ref.shape[1] // k_ref.shape[1]
    factor = scale * LOG2E
    bias = near_mask(first_seen(lens, here, rows, width), rows)
    for h in range(heads):
        n = h // share
        at = slice(h * width, (h + 1) * width)
        kv = slice(n * width, (n + 1) * width)
        k, v = k_ref[:, kv], v_ref[:, kv]
        q, g = q_ref[:, at], g_ref[:, at]
        p = jnp.exp2((dot_t(q, k) + bias) * factor - keep_ref[:, h : h + 1])
        ds = (p * (dot_t(g, v) - keep_ref[:, heads + h : heads + h + 1])).astype(jnp.bfloat16)
        dq = far_ref[:, at].astype(jnp.float32) + dot(ds, k)
        dq_ref[:, at] = (dq * scale).astype(jnp.bfloat16)
        dk_part, dv_part = dot(q.T, ds), dot(g.T, p.astype(jnp.bfloat16))
        dk, dv = (dk_part, dv_part) if h % share == 0 else (dk + dk_part, dv + dv_part)
        if h % share == share - 1:
            own_ref[:, 2 * n * width : (2 * n + 1) * width] = dk.T * scale
            own_ref[:, (2 * n + 1) * width : (2 * n + 2) * width] = dv.T


def choose_kernel(scale, place, own_ref, two_ref, four_ref, send_ref):
    even = place[0] % 2 == 0
    half = own_ref.shape[1]

    @pl.when(even)
    def _():
        send_ref[:, :half] = own_ref[...]
        send_ref[:, half:] = two_ref[...]

    @pl.when(jnp.logical_not(even))
    def _():
        send_ref[:, :half] = two_ref[...]
        send_ref[:, half:] = four_ref[...]


def join_kernel(scale, place, two_ref, four_ref, other_ref, two_out, four_out):
    even = place[0] % 2 == 0
    half = two_ref.shape[1]

    @pl.when(even)
    def _():
        three = other_ref[:, half:].astype(jnp.float32)
        two_out[...] = (two_ref[...] + three).astype(jnp.bfloat16)
        four_out[...] = four_ref[...].astype(jnp.bfloat16)

    @pl.when(jnp.logical_not(even))
    def _():
        one = other_ref[:, :half].astype(jnp.float32)
        three = other_ref[:, half:].astype(jnp.float32)
        two_out[...] = (two_ref[...] + one).astype(jnp.bfloat16)
        four_out[...] = (four_ref[...] + three).astype(jnp.bfloat16)


def total_kernel(scale, place, own_ref, other_ref, two_ref, four_ref, k_out, v_out):
    width = HEAD_WIDTH
    one = jnp.where(place[0] % 2 == 0, 1.0, 0.0)
    for n in range(k_out.shape[1] // width):
        for which, ref in enumerate((k_out, v_out)):
            at = slice((2 * n + which) * width, (2 * n + which + 1) * width)
            total = own_ref[:, at] + other_ref[:, at].astype(jnp.float32) * one
            total = total + two_ref[:, at].astype(jnp.float32) + four_ref[:, at].astype(jnp.float32)
            ref[:, n * width : (n + 1) * width] = total.astype(jnp.bfloat16)


def call(kernel, name, cost, outs, *args, scalars=0, scratch=(), hbm=()):
    whole = pl.BlockSpec(memory_space=pltpu.VMEM)
    left = pl.BlockSpec(memory_space=pltpu.HBM)
    return pl.pallas_call(
        functools.partial(kernel, 1.0 / math.sqrt(HEAD_WIDTH)),
        in_specs=[pl.BlockSpec(memory_space=pltpu.SMEM)] * scalars + [whole] * (len(args) - scalars),
        out_specs=[left if i in hbm else whole for i in range(len(outs))],
        out_shape=[
            pltpu.HBM(shape, dtype) if i in hbm else jax.ShapeDtypeStruct(shape, dtype)
            for i, (shape, dtype) in enumerate(outs)
        ],
        scratch_shapes=scratch,
        compiler_params=pltpu.CompilerParams(vmem_limit_bytes=20 << 20),
        cost_estimate=pl.CostEstimate(
            flops=cost << 20, bytes_accessed=1 << 20, transcendentals=0
        ),
        name=name,
    )(*args)


def on_device(queries, keys, values, output_gradient, lengths):
    rows, width = queries.shape[0], HEAD_WIDTH
    groups = keys.shape[1] // width
    heads = queries.shape[1] // width
    wide = 2 * groups * width
    place = lax.axis_index("seq")
    here = place.reshape(1).astype(jnp.int32)
    twos, fours, fars = [], [], []
    for own in (keys, values):
        twos.append(up(own, 2))
        fours.append(up(own, 4))
    parts, top, total, bias = call(
        own_forward_kernel,
        "own_forward",
        512,
        [(queries.shape, jnp.float32)] * 3 + [((rows, REACH * rows), jnp.float32)],
        lengths,
        here,
        queries,
        keys,
        values,
        scalars=2,
    )
    near_keys, near_values, bias = lax.optimization_barrier((keys, values, bias))
    for own, two, four in zip((near_keys, near_values), twos, fours):
        send = call(
            choose_kernel,
            "choose",
            0,
            [((rows, wide), jnp.bfloat16)],
            here,
            own,
            two,
            four,
            scalars=1,
        )[0]
        fars += [two, four, swapped(send)]
    out, dq_far, keep, two, four, odd = call(
        far_kernel,
        "far",
        6 * 1024,
        [
            (queries.shape, jnp.bfloat16),
            (queries.shape, jnp.bfloat16),
            ((rows, width), jnp.float32),
            ((rows, wide), jnp.float32),
            ((rows, wide), jnp.float32),
            ((rows, 2 * wide), jnp.bfloat16),
        ],
        queries,
        output_gradient,
        parts,
        top,
        total,
        bias,
        *fars,
        scratch=[pltpu.VMEM((groups, REACH * rows, width), jnp.bfloat16)] * 2
        + [pltpu.VMEM(queries.shape, jnp.bfloat16)] * 2
        + [pltpu.VMEM((rows, width), jnp.float32), pltpu.SemaphoreType.DMA((2 * groups + 1,))],
        hbm=(0, 1, 2),
    )
    other = swapped(odd)
    two, four = call(
        join_kernel,
        "join",
        0,
        [((rows, wide), jnp.bfloat16)] * 2,
        here,
        two,
        four,
        other,
        scalars=1,
    )
    two_back, four_back = up(two, -2), up(four, -4)
    split = lax.axis_size("head")
    got = lax.all_to_all(
        out.reshape(split, rows // split, out.shape[1]), "head", split_axis=0, concat_axis=0
    )
    keep, two = lax.optimization_barrier((keep, two))
    d_queries, own = call(
        own_backward_kernel,
        "own_backward",
        1024,
        [(queries.shape, jnp.bfloat16), ((rows, wide), jnp.float32)],
        lengths,
        here,
        queries,
        output_gradient,
        dq_far,
        keep,
        keys,
        values,
        scalars=2,
    )
    key_gradient, value_gradient = call(
        total_kernel,
        "total",
        0,
        [(keys.shape, jnp.bfloat16)] * 2,
        here,
        own,
        other,
        two_back,
        four_back,
        scalars=1,
    )
    attn_out = jnp.transpose(got, (1, 0, 2)).reshape(got.shape[1], -1)
    return (attn_out, d_queries, key_gradient, value_gradient)


def solution(mesh):
    placed = (P("seq", "head"), P("seq", "head"), P("seq", "head"), P("seq", "head"), P())
    return jax.shard_map(
        on_device,
        mesh=mesh,
        in_specs=placed,
        out_specs=(P(("seq", "head"), None), P("seq", "head"), P("seq", "head"), P("seq", "head")),
        check_vma=False,
    )
```

```python
import functools
import math

import jax
import jax.numpy as jnp
from jax import lax
from jax.experimental import pallas as pl
from jax.experimental.pallas import tpu as pltpu
from jax.sharding import PartitionSpec as P

HEAD_WIDTH = 128
REACH = 4
NEG = -1e30
LOG2E = 1.4426950408889634
PAIR = 2


def dot(a, b):
    return lax.dot_general(a, b, (((1,), (0,)), ((), ())), preferred_element_type=jnp.float32)


def dot_t(a, b):
    return lax.dot_general(a, b, (((1,), (1,)), ((), ())), preferred_element_type=jnp.float32)


def moved(value, to):
    count = lax.axis_size("seq")
    return lax.ppermute(value, "seq", [(source, to(source) % count) for source in range(count)])


def up(value, steps):
    return moved(value, lambda source: source + steps)


def swapped(value):
    return moved(value, lambda source: source ^ 1)


def first_seen(lens, here, rows, width):
    base = here[0] * rows
    row = lax.broadcasted_iota(jnp.int32, (rows, width), 0)

    def one(i, carry):
        end, start = carry
        end = end + lens[i]
        return end, jnp.where(row >= end - base, end - base, start)

    first = (jnp.int32(0), jnp.full((rows, width), -base, jnp.int32))
    return lax.fori_loop(0, lens.shape[0], one, first)[1]


def mask(start, distance):
    row = lax.broadcasted_iota(jnp.int32, start.shape, 0)
    pos = lax.broadcasted_iota(jnp.int32, start.shape, 1) - distance
    seen = pos >= start if distance >= start.shape[0] else (pos >= start) & (pos <= row)
    return jnp.where(seen, 0.0, NEG).astype(jnp.float32)


def near_mask(start, rows):
    width = start.shape[1]
    return jnp.concatenate([mask(start, -at) for at in range(0, rows, width)], axis=1)


def own_forward_kernel(
    scale, lens, here, q_ref, k_ref, v_ref, out_ref, top_ref, sum_ref, far_ref
):
    rows, width = q_ref.shape[0], HEAD_WIDTH
    start = first_seen(lens, here, rows, width)
    for at in range(0, REACH * rows, width):
        far_ref[:, at : at + width] = mask(start, REACH * rows - at)
    near = near_mask(start, rows)
    heads = q_ref.shape[1] // width
    share = q_ref.shape[1] // k_ref.shape[1]
    for h in range(heads):
        at = slice(h * width, (h + 1) * width)
        kv = slice(h // share * width, (h // share + 1) * width)
        s = dot_t(q_ref[:, at], k_ref[:, kv]) + near
        top = s.max(axis=1, keepdims=True)
        p = jnp.exp2((s - top) * (scale * LOG2E))
        top_ref[:, at] = jnp.broadcast_to(top, (rows, width))
        sum_ref[:, at] = jnp.broadcast_to(p.sum(axis=1, keepdims=True), (rows, width))
        out_ref[:, at] = dot(p.astype(jnp.bfloat16), v_ref[:, kv])


def far_kernel(scale, *refs):
    q_ref, g_ref, out_ref, top_ref, sum_ref, bias_ref = refs[0:6]
    (o_out, dq_out, keep_out, two_out, four_out, odd_out) = refs[-12:-6]
    k_all, v_all, o_ref, dq_ref, keep_ref, sent = refs[-6:]
    fars = refs[6:-12]
    rows, width = q_ref.shape[0], HEAD_WIDTH
    groups = k_all.shape[0]
    heads = q_ref.shape[1] // width
    share = heads // groups
    factor = scale * LOG2E
    bias = bias_ref[...]
    for which, to in enumerate((k_all, v_all)):
        two_ref, four_ref, odd_ref = fars[3 * which : 3 * which + 3]
        for b, (ref, place) in enumerate(((four_ref, 0), (odd_ref, 1), (two_ref, 0), (odd_ref, 0))):
            for n in range(groups):
                column = (groups * place + n) * width
                to[n, b * rows : (b + 1) * rows, :] = ref[:, column : column + width]

    def weigh(h):
        at = slice(h * width, (h + 1) * width)
        q, top = q_ref[:, at], top_ref[:, at]
        s = dot_t(q, k_all[h // share]) + bias
        most = jnp.maximum(top, s.max(axis=1, keepdims=True))
        p = jnp.exp2((s - jnp.tile(most, (1, s.shape[1] // width))) * factor)
        keep = jnp.exp2((top - most) * factor)
        total = sum_ref[:, at] * keep + p.sum(axis=1, keepdims=True)
        return at, q, p, most, keep, total

    def send(n):
        to = slice(n * share * width, (n + 1) * share * width)
        pairs = [(o_ref.at[:, to], o_out.at[:, to]), (dq_ref.at[:, to], dq_out.at[:, to])]
        if n == groups - 1:
            pairs.append((keep_ref, keep_out))
        return [pltpu.make_async_copy(*pair, sent.at[2 * n + i]) for i, pair in enumerate(pairs)]

    def settle(h, at, q, p, most, keep, total):
        inverse = 1.0 / total
        pb = p.astype(jnp.bfloat16)
        o = (dot(pb, v_all[h // share]) + out_ref[:, at] * keep) * inverse
        o_ref[:, at] = o.astype(jnp.bfloat16)
        gs = (g_ref[:, at].astype(jnp.float32) * inverse).astype(jnp.bfloat16)
        delta = jnp.sum(gs.astype(jnp.float32) * o, axis=1, keepdims=True)
        keep_ref[:, h : h + 1] = most[:, :1] * factor + jnp.log2(total[:, :1])
        keep_ref[:, heads + h : heads + h + 1] = delta * total[:, :1]
        return h, at, q, p, pb, gs, delta

    def differ(h, at, q, p, pb, gs, delta):
        ds = (p * (dot_t(gs, v_all[h // share]) - delta)).astype(jnp.bfloat16)
        dq_ref[:, at] = dot(ds, k_all[h // share]).astype(jnp.bfloat16)
        return q, gs, ds, pb

    weighed, settled, held = weigh(0), None, []
    for h in range(heads + 1):
        ahead = weigh(h + 1) if h + 1 < heads else None
        done = settle(h, *weighed) if h < heads else None
        if settled is not None:
            held.append(differ(*settled))
            if len(held) == PAIR:
                q, gs, ds, pb = (jnp.concatenate(x, axis=0) for x in zip(*held))
                held = []
                dk_part, dv_part = dot(q.T, ds), dot(gs.T, pb)
                if h % share == PAIR:
                    dk, dv = dk_part, dv_part
                else:
                    dk, dv = dk + dk_part, dv + dv_part
            if h % share == 0:
                n = h // share - 1
                for copy in send(n):
                    copy.start()
                outs = ((four_out, 0), (odd_out, 1), (two_out, 0), (odd_out, 0))
                for b, (ref, place) in enumerate(outs):
                    at = slice(b * rows, (b + 1) * rows)
                    for which, grad in enumerate((dk[:, at].T * scale, dv[:, at].T)):
                        to = (2 * groups * place + 2 * n + which) * width
                        ref[:, to : to + width] = grad.astype(ref.dtype)
        weighed, settled = ahead, done
    for n in range(groups):
        for copy in send(n):
            copy.wait()


def own_backward_kernel(
    scale, lens, here, q_ref, g_ref, far_ref, keep_ref, k_ref, v_ref, dq_ref, own_ref
):
    rows, width = q_ref.shape[0], HEAD_WIDTH
    heads = q_ref.shape[1] // width
    share = q_ref.shape[1] // k_ref.shape[1]
    factor = scale * LOG2E
    bias = near_mask(first_seen(lens, here, rows, width), rows)
    for h in range(heads):
        n = h // share
        at = slice(h * width, (h + 1) * width)
        kv = slice(n * width, (n + 1) * width)
        k, v = k_ref[:, kv], v_ref[:, kv]
        q, g = q_ref[:, at], g_ref[:, at]
        p = jnp.exp2((dot_t(q, k) + bias) * factor - keep_ref[:, h : h + 1])
        ds = (p * (dot_t(g, v) - keep_ref[:, heads + h : heads + h + 1])).astype(jnp.bfloat16)
        dq = far_ref[:, at].astype(jnp.float32) + dot(ds, k)
        dq_ref[:, at] = (dq * scale).astype(jnp.bfloat16)
        dk_part, dv_part = dot(q.T, ds), dot(g.T, p.astype(jnp.bfloat16))
        dk, dv = (dk_part, dv_part) if h % share == 0 else (dk + dk_part, dv + dv_part)
        if h % share == share - 1:
            own_ref[:, 2 * n * width : (2 * n + 1) * width] = dk.T * scale
            own_ref[:, (2 * n + 1) * width : (2 * n + 2) * width] = dv.T


def choose_kernel(scale, place, own_ref, two_ref, four_ref, send_ref):
    even = place[0] % 2 == 0
    half = own_ref.shape[1]

    @pl.when(even)
    def _():
        send_ref[:, :half] = own_ref[...]
        send_ref[:, half:] = two_ref[...]

    @pl.when(jnp.logical_not(even))
    def _():
        send_ref[:, :half] = two_ref[...]
        send_ref[:, half:] = four_ref[...]


def join_kernel(scale, place, two_ref, four_ref, other_ref, two_out, four_out):
    even = place[0] % 2 == 0
    half = two_ref.shape[1]

    @pl.when(even)
    def _():
        three = other_ref[:, half:].astype(jnp.float32)
        two_out[...] = (two_ref[...] + three).astype(jnp.bfloat16)
        four_out[...] = four_ref[...].astype(jnp.bfloat16)

    @pl.when(jnp.logical_not(even))
    def _():
        one = other_ref[:, :half].astype(jnp.float32)
        three = other_ref[:, half:].astype(jnp.float32)
        two_out[...] = (two_ref[...] + one).astype(jnp.bfloat16)
        four_out[...] = (four_ref[...] + three).astype(jnp.bfloat16)


def total_kernel(scale, place, own_ref, other_ref, two_ref, four_ref, k_out, v_out):
    width = HEAD_WIDTH
    one = jnp.where(place[0] % 2 == 0, 1.0, 0.0)
    for n in range(k_out.shape[1] // width):
        for which, ref in enumerate((k_out, v_out)):
            at = slice((2 * n + which) * width, (2 * n + which + 1) * width)
            total = own_ref[:, at] + other_ref[:, at].astype(jnp.float32) * one
            total = total + two_ref[:, at].astype(jnp.float32) + four_ref[:, at].astype(jnp.float32)
            ref[:, n * width : (n + 1) * width] = total.astype(jnp.bfloat16)


def call(kernel, name, cost, outs, *args, scalars=0, scratch=(), hbm=()):
    whole = pl.BlockSpec(memory_space=pltpu.VMEM)
    left = pl.BlockSpec(memory_space=pltpu.HBM)
    return pl.pallas_call(
        functools.partial(kernel, 1.0 / math.sqrt(HEAD_WIDTH)),
        in_specs=[pl.BlockSpec(memory_space=pltpu.SMEM)] * scalars + [whole] * (len(args) - scalars),
        out_specs=[left if i in hbm else whole for i in range(len(outs))],
        out_shape=[
            pltpu.HBM(shape, dtype) if i in hbm else jax.ShapeDtypeStruct(shape, dtype)
            for i, (shape, dtype) in enumerate(outs)
        ],
        scratch_shapes=scratch,
        compiler_params=pltpu.CompilerParams(vmem_limit_bytes=20 << 20),
        cost_estimate=pl.CostEstimate(
            flops=cost << 20, bytes_accessed=1 << 20, transcendentals=0
        ),
        name=name,
    )(*args)


def on_device(queries, keys, values, output_gradient, lengths):
    rows, width = queries.shape[0], HEAD_WIDTH
    groups = keys.shape[1] // width
    heads = queries.shape[1] // width
    wide = 2 * groups * width
    place = lax.axis_index("seq")
    here = place.reshape(1).astype(jnp.int32)
    twos, fours, fars = [], [], []
    for own in (keys, values):
        twos.append(up(own, 2))
        fours.append(up(own, 4))
    parts, top, total, bias = call(
        own_forward_kernel,
        "own_forward",
        512,
        [(queries.shape, jnp.float32)] * 3 + [((rows, REACH * rows), jnp.float32)],
        lengths,
        here,
        queries,
        keys,
        values,
        scalars=2,
    )
    near_keys, near_values, bias = lax.optimization_barrier((keys, values, bias))
    for own, two, four in zip((near_keys, near_values), twos, fours):
        send = call(
            choose_kernel,
            "choose",
            0,
            [((rows, wide), jnp.bfloat16)],
            here,
            own,
            two,
            four,
            scalars=1,
        )[0]
        fars += [two, four, swapped(send)]
    out, dq_far, keep, two, four, odd = call(
        far_kernel,
        "far",
        6 * 1024,
        [
            (queries.shape, jnp.bfloat16),
            (queries.shape, jnp.bfloat16),
            ((rows, width), jnp.float32),
            ((rows, wide), jnp.float32),
            ((rows, wide), jnp.float32),
            ((rows, 2 * wide), jnp.bfloat16),
        ],
        queries,
        output_gradient,
        parts,
        top,
        total,
        bias,
        *fars,
        scratch=[pltpu.VMEM((groups, REACH * rows, width), jnp.bfloat16)] * 2
        + [pltpu.VMEM(queries.shape, jnp.bfloat16)] * 2
        + [pltpu.VMEM((rows, width), jnp.float32), pltpu.SemaphoreType.DMA((2 * groups + 1,))],
        hbm=(0, 1, 2),
    )
    other = swapped(odd)
    two, four = call(
        join_kernel,
        "join",
        0,
        [((rows, wide), jnp.bfloat16)] * 2,
        here,
        two,
        four,
        other,
        scalars=1,
    )
    two_back, four_back = up(two, -2), up(four, -4)
    split = lax.axis_size("head")
    got = lax.all_to_all(
        out.reshape(split, rows // split, out.shape[1]), "head", split_axis=0, concat_axis=0
    )
    keep, two = lax.optimization_barrier((keep, two))
    d_queries, own = call(
        own_backward_kernel,
        "own_backward",
        1024,
        [(queries.shape, jnp.bfloat16), ((rows, wide), jnp.float32)],
        lengths,
        here,
        queries,
        output_gradient,
        dq_far,
        keep,
        keys,
        values,
        scalars=2,
    )
    key_gradient, value_gradient = call(
        total_kernel,
        "total",
        0,
        [(keys.shape, jnp.bfloat16)] * 2,
        here,
        own,
        other,
        two_back,
        four_back,
        scalars=1,
    )
    attn_out = jnp.transpose(got, (1, 0, 2)).reshape(got.shape[1], -1)
    return (attn_out, d_queries, key_gradient, value_gradient)


def solution(mesh):
    placed = (P("seq", "head"), P("seq", "head"), P("seq", "head"), P("seq", "head"), P())
    return jax.shard_map(
        on_device,
        mesh=mesh,
        in_specs=placed,
        out_specs=(P(("seq", "head"), None), P("seq", "head"), P("seq", "head"), P("seq", "head")),
        check_vma=False,
    )
```

```python
import functools
import math

import jax
import jax.numpy as jnp
from jax import lax
from jax.experimental import pallas as pl
from jax.experimental.pallas import tpu as pltpu
from jax.sharding import PartitionSpec as P

HEAD_WIDTH = 128
REACH = 4
NEG = -1e30
LOG2E = 1.4426950408889634
PAIR = 2


def dot(a, b):
    return lax.dot_general(a, b, (((1,), (0,)), ((), ())), preferred_element_type=jnp.float32)


def dot_t(a, b):
    return lax.dot_general(a, b, (((1,), (1,)), ((), ())), preferred_element_type=jnp.float32)


def moved(value, to):
    count = lax.axis_size("seq")
    return lax.ppermute(value, "seq", [(source, to(source) % count) for source in range(count)])


def up(value, steps):
    return moved(value, lambda source: source + steps)


def swapped(value):
    return moved(value, lambda source: source ^ 1)


def first_seen(lens, here, rows, width):
    base = here[0] * rows
    row = lax.broadcasted_iota(jnp.int32, (rows, width), 0)

    def one(i, carry):
        end, start = carry
        end = end + lens[i]
        return end, jnp.where(row >= end - base, end - base, start)

    first = (jnp.int32(0), jnp.full((rows, width), -base, jnp.int32))
    return lax.fori_loop(0, lens.shape[0], one, first)[1]


def mask(start, distance):
    row = lax.broadcasted_iota(jnp.int32, start.shape, 0)
    pos = lax.broadcasted_iota(jnp.int32, start.shape, 1) - distance
    seen = pos >= start if distance >= start.shape[0] else (pos >= start) & (pos <= row)
    return jnp.where(seen, 0.0, NEG).astype(jnp.float32)


def near_mask(start, rows):
    width = start.shape[1]
    return jnp.concatenate([mask(start, -at) for at in range(0, rows, width)], axis=1)


def own_forward_kernel(
    scale, lens, here, q_ref, k_ref, v_ref, out_ref, top_ref, sum_ref, far_ref
):
    rows, width = q_ref.shape[0], HEAD_WIDTH
    start = first_seen(lens, here, rows, width)
    for at in range(0, REACH * rows, width):
        far_ref[:, at : at + width] = mask(start, REACH * rows - at)
    near = near_mask(start, rows)
    heads = q_ref.shape[1] // width
    share = q_ref.shape[1] // k_ref.shape[1]
    for h in range(heads):
        at = slice(h * width, (h + 1) * width)
        kv = slice(h // share * width, (h // share + 1) * width)
        s = dot_t(q_ref[:, at], k_ref[:, kv]) + near
        top = s.max(axis=1, keepdims=True)
        p = jnp.exp2((s - top) * (scale * LOG2E))
        top_ref[:, at] = jnp.broadcast_to(top, (rows, width))
        sum_ref[:, at] = jnp.broadcast_to(p.sum(axis=1, keepdims=True), (rows, width))
        out_ref[:, at] = dot(p.astype(jnp.bfloat16), v_ref[:, kv])


def far_kernel(split, scale, turn, *refs):
    q_ref, g_ref, out_ref, top_ref, sum_ref, bias_ref = refs[0:6]
    o_outs = refs[-11 - split : -11]
    dq_out, keep_out, two_out, four_out, odd_out = refs[-11:-6]
    k_all, v_all, o_ref, dq_ref, keep_ref, sent = refs[-6:]
    fars = refs[6 : -11 - split]
    rows, width = q_ref.shape[0], HEAD_WIDTH
    groups = k_all.shape[0]
    heads = q_ref.shape[1] // width
    share = heads // groups
    factor = scale * LOG2E
    bias = bias_ref[...]
    for which, to in enumerate((k_all, v_all)):
        two_ref, four_ref, odd_ref = fars[3 * which : 3 * which + 3]
        for b, (ref, place) in enumerate(((four_ref, 0), (odd_ref, 1), (two_ref, 0), (odd_ref, 0))):
            for n in range(groups):
                column = (groups * place + n) * width
                to[n, b * rows : (b + 1) * rows, :] = ref[:, column : column + width]

    def weigh(h):
        at = slice(h * width, (h + 1) * width)
        q, top = q_ref[:, at], top_ref[:, at]
        s = dot_t(q, k_all[h // share]) + bias
        most = jnp.maximum(top, s.max(axis=1, keepdims=True))
        p = jnp.exp2((s - jnp.tile(most, (1, s.shape[1] // width))) * factor)
        keep = jnp.exp2((top - most) * factor)
        total = sum_ref[:, at] * keep + p.sum(axis=1, keepdims=True)
        return at, q, p, most, keep, total

    def send(n):
        to = slice(n * share * width, (n + 1) * share * width)
        piece = rows // split
        pairs = [(dq_ref.at[:, to], dq_out.at[:, to])]
        for ahead, o_out in enumerate(o_outs):
            first = pl.multiple_of(lax.rem(turn[0] + ahead, split) * piece, piece)
            pairs.append((o_ref.at[pl.ds(first, piece), to], o_out.at[:, to]))
        if n == groups - 1:
            pairs.append((keep_ref, keep_out))
        first = n * (split + 1)
        return [pltpu.make_async_copy(*pair, sent.at[first + i]) for i, pair in enumerate(pairs)]

    def settle(h, at, q, p, most, keep, total):
        inverse = 1.0 / total
        pb = p.astype(jnp.bfloat16)
        o = (dot(pb, v_all[h // share]) + out_ref[:, at] * keep) * inverse
        o_ref[:, at] = o.astype(jnp.bfloat16)
        gs = (g_ref[:, at].astype(jnp.float32) * inverse).astype(jnp.bfloat16)
        delta = jnp.sum(gs.astype(jnp.float32) * o, axis=1, keepdims=True)
        keep_ref[:, h : h + 1] = most[:, :1] * factor + jnp.log2(total[:, :1])
        keep_ref[:, heads + h : heads + h + 1] = delta * total[:, :1]
        return h, at, q, p, pb, gs, delta

    def differ(h, at, q, p, pb, gs, delta):
        ds = (p * (dot_t(gs, v_all[h // share]) - delta)).astype(jnp.bfloat16)
        dq_ref[:, at] = dot(ds, k_all[h // share]).astype(jnp.bfloat16)
        return q, gs, ds, pb

    weighed, settled, held = weigh(0), None, []
    for h in range(heads + 1):
        ahead = weigh(h + 1) if h + 1 < heads else None
        done = settle(h, *weighed) if h < heads else None
        if settled is not None:
            held.append(differ(*settled))
            if len(held) == PAIR:
                q, gs, ds, pb = (jnp.concatenate(x, axis=0) for x in zip(*held))
                held = []
                dk_part, dv_part = dot(q.T, ds), dot(gs.T, pb)
                if h % share == PAIR:
                    dk, dv = dk_part, dv_part
                else:
                    dk, dv = dk + dk_part, dv + dv_part
            if h % share == 0:
                n = h // share - 1
                for copy in send(n):
                    copy.start()
                outs = ((four_out, 0), (odd_out, 1), (two_out, 0), (odd_out, 0))
                for b, (ref, place) in enumerate(outs):
                    at = slice(b * rows, (b + 1) * rows)
                    for which, grad in enumerate((dk[:, at].T * scale, dv[:, at].T)):
                        to = (2 * groups * place + 2 * n + which) * width
                        ref[:, to : to + width] = grad.astype(ref.dtype)
        weighed, settled = ahead, done
    for n in range(groups):
        for copy in send(n):
            copy.wait()


def own_backward_kernel(
    scale, lens, here, q_ref, g_ref, far_ref, keep_ref, k_ref, v_ref, dq_ref, own_ref
):
    rows, width = q_ref.shape[0], HEAD_WIDTH
    heads = q_ref.shape[1] // width
    share = q_ref.shape[1] // k_ref.shape[1]
    factor = scale * LOG2E
    bias = near_mask(first_seen(lens, here, rows, width), rows)
    for h in range(heads):
        n = h // share
        at = slice(h * width, (h + 1) * width)
        kv = slice(n * width, (n + 1) * width)
        k, v = k_ref[:, kv], v_ref[:, kv]
        q, g = q_ref[:, at], g_ref[:, at]
        p = jnp.exp2((dot_t(q, k) + bias) * factor - keep_ref[:, h : h + 1])
        ds = (p * (dot_t(g, v) - keep_ref[:, heads + h : heads + h + 1])).astype(jnp.bfloat16)
        dq = far_ref[:, at].astype(jnp.float32) + dot(ds, k)
        dq_ref[:, at] = (dq * scale).astype(jnp.bfloat16)
        dk_part, dv_part = dot(q.T, ds), dot(g.T, p.astype(jnp.bfloat16))
        dk, dv = (dk_part, dv_part) if h % share == 0 else (dk + dk_part, dv + dv_part)
        if h % share == share - 1:
            own_ref[:, 2 * n * width : (2 * n + 1) * width] = dk.T * scale
            own_ref[:, (2 * n + 1) * width : (2 * n + 2) * width] = dv.T


def choose_kernel(scale, place, own_ref, two_ref, four_ref, send_ref):
    even = place[0] % 2 == 0
    half = own_ref.shape[1]

    @pl.when(even)
    def _():
        send_ref[:, :half] = own_ref[...]
        send_ref[:, half:] = two_ref[...]

    @pl.when(jnp.logical_not(even))
    def _():
        send_ref[:, :half] = two_ref[...]
        send_ref[:, half:] = four_ref[...]


def join_kernel(scale, place, two_ref, four_ref, other_ref, two_out, four_out):
    even = place[0] % 2 == 0
    half = two_ref.shape[1]

    @pl.when(even)
    def _():
        three = other_ref[:, half:].astype(jnp.float32)
        two_out[...] = (two_ref[...] + three).astype(jnp.bfloat16)
        four_out[...] = four_ref[...].astype(jnp.bfloat16)

    @pl.when(jnp.logical_not(even))
    def _():
        one = other_ref[:, :half].astype(jnp.float32)
        three = other_ref[:, half:].astype(jnp.float32)
        two_out[...] = (two_ref[...] + one).astype(jnp.bfloat16)
        four_out[...] = (four_ref[...] + three).astype(jnp.bfloat16)


def spread_kernel(scale, turn, *refs):
    pieces, out_ref, sent = refs[:-2], refs[-2], refs[-1]
    split, cols = len(pieces), pieces[0].shape[1]
    copies = []
    for ahead, piece in enumerate(pieces):
        first = pl.multiple_of(lax.rem(turn[0] + split - ahead, split) * cols, cols)
        copies.append(pltpu.make_async_copy(piece, out_ref.at[:, pl.ds(first, cols)], sent.at[ahead]))
        copies[-1].start()
    for copy in copies:
        copy.wait()


def total_kernel(scale, place, own_ref, other_ref, two_ref, four_ref, k_out, v_out):
    width = HEAD_WIDTH
    one = jnp.where(place[0] % 2 == 0, 1.0, 0.0)
    for n in range(k_out.shape[1] // width):
        for which, ref in enumerate((k_out, v_out)):
            at = slice((2 * n + which) * width, (2 * n + which + 1) * width)
            total = own_ref[:, at] + other_ref[:, at].astype(jnp.float32) * one
            total = total + two_ref[:, at].astype(jnp.float32) + four_ref[:, at].astype(jnp.float32)
            ref[:, n * width : (n + 1) * width] = total.astype(jnp.bfloat16)


def call(kernel, name, cost, outs, *args, scalars=0, scratch=(), hbm=(), stay=0):
    whole = pl.BlockSpec(memory_space=pltpu.VMEM)
    left = pl.BlockSpec(memory_space=pltpu.HBM)
    return pl.pallas_call(
        functools.partial(kernel, 1.0 / math.sqrt(HEAD_WIDTH)),
        in_specs=[pl.BlockSpec(memory_space=pltpu.SMEM)] * scalars
        + [whole] * (len(args) - scalars - stay)
        + [pl.BlockSpec(memory_space=pl.ANY)] * stay,
        out_specs=[left if i in hbm else whole for i in range(len(outs))],
        out_shape=[
            pltpu.HBM(shape, dtype) if i in hbm else jax.ShapeDtypeStruct(shape, dtype)
            for i, (shape, dtype) in enumerate(outs)
        ],
        scratch_shapes=scratch,
        compiler_params=pltpu.CompilerParams(vmem_limit_bytes=20 << 20),
        cost_estimate=pl.CostEstimate(
            flops=cost << 20, bytes_accessed=1 << 20, transcendentals=0
        ),
        name=name,
    )(*args)


def on_device(queries, keys, values, output_gradient, lengths):
    rows, width = queries.shape[0], HEAD_WIDTH
    groups = keys.shape[1] // width
    heads = queries.shape[1] // width
    wide = 2 * groups * width
    place = lax.axis_index("seq")
    here = place.reshape(1).astype(jnp.int32)
    turn = lax.axis_index("head").reshape(1).astype(jnp.int32)
    split = lax.axis_size("head")
    twos, fours, fars = [], [], []
    for own in (keys, values):
        twos.append(up(own, 2))
        fours.append(up(own, 4))
    parts, top, total, bias = call(
        own_forward_kernel,
        "own_forward",
        512,
        [(queries.shape, jnp.float32)] * 3 + [((rows, REACH * rows), jnp.float32)],
        lengths,
        here,
        queries,
        keys,
        values,
        scalars=2,
    )
    near_keys, near_values, bias = lax.optimization_barrier((keys, values, bias))
    for own, two, four in zip((near_keys, near_values), twos, fours):
        send = call(
            choose_kernel,
            "choose",
            0,
            [((rows, wide), jnp.bfloat16)],
            here,
            own,
            two,
            four,
            scalars=1,
        )[0]
        fars += [two, four, swapped(send)]
    *pieces, dq_far, keep, two, four, odd = call(
        functools.partial(far_kernel, split),
        "far",
        6 * 1024,
        [((rows // split, queries.shape[1]), jnp.bfloat16)] * split
        + [
            (queries.shape, jnp.bfloat16),
            ((rows, width), jnp.float32),
            ((rows, wide), jnp.float32),
            ((rows, wide), jnp.float32),
            ((rows, 2 * wide), jnp.bfloat16),
        ],
        turn,
        queries,
        output_gradient,
        parts,
        top,
        total,
        bias,
        *fars,
        scratch=[pltpu.VMEM((groups, REACH * rows, width), jnp.bfloat16)] * 2
        + [pltpu.VMEM(queries.shape, jnp.bfloat16)] * 2
        + [pltpu.VMEM((rows, width), jnp.float32), pltpu.SemaphoreType.DMA((groups * (split + 1) + 1,))],
        scalars=1,
        hbm=range(split + 2),
    )
    other = swapped(odd)
    two, four = call(
        join_kernel,
        "join",
        0,
        [((rows, wide), jnp.bfloat16)] * 2,
        here,
        two,
        four,
        other,
        scalars=1,
    )
    two_back, four_back = up(two, -2), up(four, -4)

    def around(piece, ahead):
        return lax.ppermute(
            piece, "head", [(source, (source + ahead) % split) for source in range(split)]
        )

    late, two = lax.optimization_barrier((pieces, two))
    got = [around(pieces[n] if n == split // 2 else late[n], n) for n in range(1, split)]
    keep, two = lax.optimization_barrier((keep, two))
    d_queries, own = call(
        own_backward_kernel,
        "own_backward",
        1024,
        [(queries.shape, jnp.bfloat16), ((rows, wide), jnp.float32)],
        lengths,
        here,
        queries,
        output_gradient,
        dq_far,
        keep,
        keys,
        values,
        scalars=2,
    )
    key_gradient, value_gradient = call(
        total_kernel,
        "total",
        0,
        [(keys.shape, jnp.bfloat16)] * 2,
        here,
        own,
        other,
        two_back,
        four_back,
        scalars=1,
    )
    got, key_gradient = lax.optimization_barrier((got, key_gradient))
    attn_out = call(
        spread_kernel,
        "spread",
        0,
        [((rows // split, split * queries.shape[1]), jnp.bfloat16)],
        turn,
        pieces[0],
        *got,
        scalars=1,
        scratch=[pltpu.SemaphoreType.DMA((split,))],
        hbm=(0,),
        stay=split,
    )[0]
    return (attn_out, d_queries, key_gradient, value_gradient)


def solution(mesh):
    placed = (P("seq", "head"), P("seq", "head"), P("seq", "head"), P("seq", "head"), P())
    return jax.shard_map(
        on_device,
        mesh=mesh,
        in_specs=placed,
        out_specs=(P(("seq", "head"), None), P("seq", "head"), P("seq", "head"), P("seq", "head")),
        check_vma=False,
    )
```

```python
import functools
import math

import jax
import jax.numpy as jnp
from jax import lax
from jax.experimental import pallas as pl
from jax.experimental.pallas import tpu as pltpu
from jax.sharding import PartitionSpec as P

HEAD_WIDTH = 128
REACH = 4
NEG = -1e30
LOG2E = 1.4426950408889634
PAIR = 4


def dot(a, b):
    return lax.dot_general(a, b, (((1,), (0,)), ((), ())), preferred_element_type=jnp.float32)


def dot_t(a, b):
    return lax.dot_general(a, b, (((1,), (1,)), ((), ())), preferred_element_type=jnp.float32)


def moved(value, to):
    count = lax.axis_size("seq")
    return lax.ppermute(value, "seq", [(source, to(source) % count) for source in range(count)])


def up(value, steps):
    return moved(value, lambda source: source + steps)


def swapped(value):
    return moved(value, lambda source: source ^ 1)


def first_seen(lens, here, rows, width):
    base = here[0] * rows
    row = lax.broadcasted_iota(jnp.int32, (rows, width), 0)

    def one(i, carry):
        end, start = carry
        end = end + lens[i]
        return end, jnp.where(row >= end - base, end - base, start)

    first = (jnp.int32(0), jnp.full((rows, width), -base, jnp.int32))
    return lax.fori_loop(0, lens.shape[0], one, first)[1]


def mask(start, distance):
    row = lax.broadcasted_iota(jnp.int32, start.shape, 0)
    pos = lax.broadcasted_iota(jnp.int32, start.shape, 1) - distance
    seen = pos >= start if distance >= start.shape[0] else (pos >= start) & (pos <= row)
    return jnp.where(seen, 0.0, NEG).astype(jnp.float32)


def near_mask(start, rows):
    width = start.shape[1]
    return jnp.concatenate([mask(start, -at) for at in range(0, rows, width)], axis=1)


def own_forward_kernel(
    scale, lens, here, q_ref, k_ref, v_ref, out_ref, top_ref, sum_ref, far_ref
):
    rows, width = q_ref.shape[0], HEAD_WIDTH
    start = first_seen(lens, here, rows, width)
    for at in range(0, REACH * rows, width):
        far_ref[:, at : at + width] = mask(start, REACH * rows - at)
    near = near_mask(start, rows)
    heads = q_ref.shape[1] // width
    share = q_ref.shape[1] // k_ref.shape[1]
    for h in range(heads):
        at = slice(h * width, (h + 1) * width)
        kv = slice(h // share * width, (h // share + 1) * width)
        s = dot_t(q_ref[:, at], k_ref[:, kv]) + near
        top = s.max(axis=1, keepdims=True)
        p = jnp.exp2((s - top) * (scale * LOG2E))
        top_ref[:, at] = jnp.broadcast_to(top, (rows, width))
        sum_ref[:, at] = jnp.broadcast_to(p.sum(axis=1, keepdims=True), (rows, width))
        out_ref[:, at] = dot(p.astype(jnp.bfloat16), v_ref[:, kv])


def far_kernel(scale, *refs):
    q_ref, g_ref, out_ref, top_ref, sum_ref, bias_ref = refs[0:6]
    (o_out, dq_out, keep_out, two_out, four_out, odd_out) = refs[-12:-6]
    k_all, v_all, o_ref, dq_ref, keep_ref, sent = refs[-6:]
    fars = refs[6:-12]
    rows, width = q_ref.shape[0], HEAD_WIDTH
    groups = k_all.shape[0]
    heads = q_ref.shape[1] // width
    share = heads // groups
    factor = scale * LOG2E
    bias = bias_ref[...]
    for which, to in enumerate((k_all, v_all)):
        four_ref, two_ref, odd_ref = fars[3 * which : 3 * which + 3]
        for b, (ref, place) in enumerate(((four_ref, 0), (odd_ref, 1), (two_ref, 0), (odd_ref, 0))):
            for n in range(groups):
                column = (groups * place + n) * width
                to[n, b * rows : (b + 1) * rows, :] = ref[:, column : column + width]

    def weigh(h):
        at = slice(h * width, (h + 1) * width)
        q, top = q_ref[:, at], top_ref[:, at]
        s = dot_t(q, k_all[h // share]) + bias
        most = jnp.maximum(top, s.max(axis=1, keepdims=True))
        p = jnp.exp2((s - jnp.tile(most, (1, s.shape[1] // width))) * factor)
        keep = jnp.exp2((top - most) * factor)
        total = sum_ref[:, at] * keep + p.sum(axis=1, keepdims=True)
        return at, q, p, most, keep, total

    def send(n):
        to = slice(n * share * width, (n + 1) * share * width)
        pairs = [(o_ref.at[:, to], o_out.at[:, to]), (dq_ref.at[:, to], dq_out.at[:, to])]
        if n == groups - 1:
            pairs.append((keep_ref, keep_out))
        return [pltpu.make_async_copy(*pair, sent.at[2 * n + i]) for i, pair in enumerate(pairs)]

    def settle(h, at, q, p, most, keep, total):
        inverse = 1.0 / total
        pb = p.astype(jnp.bfloat16)
        o = (dot(pb, v_all[h // share]) + out_ref[:, at] * keep) * inverse
        o_ref[:, at] = o.astype(jnp.bfloat16)
        gs = (g_ref[:, at].astype(jnp.float32) * inverse).astype(jnp.bfloat16)
        delta = jnp.sum(gs.astype(jnp.float32) * o, axis=1, keepdims=True)
        keep_ref[:, h : h + 1] = most[:, :1] * factor + jnp.log2(total[:, :1])
        keep_ref[:, heads + h : heads + h + 1] = delta * total[:, :1]
        return h, at, q, p, pb, gs, delta

    def differ(h, at, q, p, pb, gs, delta):
        ds = (p * (dot_t(gs, v_all[h // share]) - delta)).astype(jnp.bfloat16)
        dq_ref[:, at] = dot(ds, k_all[h // share]).astype(jnp.bfloat16)
        return q, gs, ds, pb

    weighed, settled, held = weigh(0), None, []
    for h in range(heads + 1):
        ahead = weigh(h + 1) if h + 1 < heads else None
        done = settle(h, *weighed) if h < heads else None
        if settled is not None:
            held.append(differ(*settled))
            if len(held) == PAIR:
                q, gs, ds, pb = (jnp.concatenate(x, axis=0) for x in zip(*held))
                held = []
                dk_part, dv_part = dot(q.T, ds), dot(gs.T, pb)
                if h % share == PAIR:
                    dk, dv = dk_part, dv_part
                else:
                    dk, dv = dk + dk_part, dv + dv_part
            if h % share == 0:
                n = h // share - 1
                for copy in send(n):
                    copy.start()
                outs = ((four_out, 0), (odd_out, 1), (two_out, 0), (odd_out, 0))
                for b, (ref, place) in enumerate(outs):
                    at = slice(b * rows, (b + 1) * rows)
                    for which, grad in enumerate((dk[:, at].T * scale, dv[:, at].T)):
                        to = (2 * groups * place + 2 * n + which) * width
                        ref[:, to : to + width] = grad.astype(ref.dtype)
        weighed, settled = ahead, done
    for n in range(groups):
        for copy in send(n):
            copy.wait()


def own_backward_kernel(
    scale, lens, here, q_ref, g_ref, far_ref, keep_ref, k_ref, v_ref, dq_ref, own_ref
):
    rows, width = q_ref.shape[0], HEAD_WIDTH
    heads = q_ref.shape[1] // width
    share = q_ref.shape[1] // k_ref.shape[1]
    factor = scale * LOG2E
    bias = near_mask(first_seen(lens, here, rows, width), rows)
    for h in range(heads):
        n = h // share
        at = slice(h * width, (h + 1) * width)
        kv = slice(n * width, (n + 1) * width)
        k, v = k_ref[:, kv], v_ref[:, kv]
        q, g = q_ref[:, at], g_ref[:, at]
        p = jnp.exp2((dot_t(q, k) + bias) * factor - keep_ref[:, h : h + 1])
        ds = (p * (dot_t(g, v) - keep_ref[:, heads + h : heads + h + 1])).astype(jnp.bfloat16)
        dq = far_ref[:, at].astype(jnp.float32) + dot(ds, k)
        dq_ref[:, at] = (dq * scale).astype(jnp.bfloat16)
        dk_part, dv_part = dot(q.T, ds), dot(g.T, p.astype(jnp.bfloat16))
        dk, dv = (dk_part, dv_part) if h % share == 0 else (dk + dk_part, dv + dv_part)
        if h % share == share - 1:
            own_ref[:, 2 * n * width : (2 * n + 1) * width] = dk.T * scale
            own_ref[:, (2 * n + 1) * width : (2 * n + 2) * width] = dv.T


def choose_kernel(scale, place, own_ref, four_ref, two_ref, send_ref):
    even = place[0] % 2 == 0
    half = own_ref.shape[1]

    @pl.when(even)
    def _():
        send_ref[:, :half] = own_ref[...]
        send_ref[:, half:] = two_ref[...]

    @pl.when(jnp.logical_not(even))
    def _():
        send_ref[:, :half] = two_ref[...]
        send_ref[:, half:] = four_ref[...]


def join_kernel(scale, place, two_ref, four_ref, other_ref, two_out, four_out):
    even = place[0] % 2 == 0
    half = two_ref.shape[1]

    @pl.when(even)
    def _():
        three = other_ref[:, half:].astype(jnp.float32)
        two_out[...] = (two_ref[...] + three).astype(jnp.bfloat16)
        four_out[...] = four_ref[...].astype(jnp.bfloat16)

    @pl.when(jnp.logical_not(even))
    def _():
        one = other_ref[:, :half].astype(jnp.float32)
        three = other_ref[:, half:].astype(jnp.float32)
        two_out[...] = (two_ref[...] + one).astype(jnp.bfloat16)
        four_out[...] = (four_ref[...] + three).astype(jnp.bfloat16)


def total_kernel(scale, place, own_ref, other_ref, two_ref, four_ref, k_out, v_out):
    width = HEAD_WIDTH
    one = jnp.where(place[0] % 2 == 0, 1.0, 0.0)
    for n in range(k_out.shape[1] // width):
        for which, ref in enumerate((k_out, v_out)):
            at = slice((2 * n + which) * width, (2 * n + which + 1) * width)
            total = own_ref[:, at] + other_ref[:, at].astype(jnp.float32) * one
            total = total + two_ref[:, at].astype(jnp.float32) + four_ref[:, at].astype(jnp.float32)
            ref[:, n * width : (n + 1) * width] = total.astype(jnp.bfloat16)


def call(kernel, name, cost, outs, *args, scalars=0, scratch=(), hbm=()):
    whole = pl.BlockSpec(memory_space=pltpu.VMEM)
    left = pl.BlockSpec(memory_space=pltpu.HBM)
    return pl.pallas_call(
        functools.partial(kernel, 1.0 / math.sqrt(HEAD_WIDTH)),
        in_specs=[pl.BlockSpec(memory_space=pltpu.SMEM)] * scalars + [whole] * (len(args) - scalars),
        out_specs=[left if i in hbm else whole for i in range(len(outs))],
        out_shape=[
            pltpu.HBM(shape, dtype) if i in hbm else jax.ShapeDtypeStruct(shape, dtype)
            for i, (shape, dtype) in enumerate(outs)
        ],
        scratch_shapes=scratch,
        compiler_params=pltpu.CompilerParams(vmem_limit_bytes=20 << 20),
        cost_estimate=pl.CostEstimate(
            flops=cost << 20, bytes_accessed=1 << 20, transcendentals=0
        ),
        name=name,
    )(*args)


def on_device(queries, keys, values, output_gradient, lengths):
    rows, width = queries.shape[0], HEAD_WIDTH
    groups = keys.shape[1] // width
    heads = queries.shape[1] // width
    wide = 2 * groups * width
    place = lax.axis_index("seq")
    here = place.reshape(1).astype(jnp.int32)
    twos, fours, fars = [], [], []
    for own in (keys, values):
        fours.append(up(own, 4))
    for own in (keys, values):
        twos.append(up(own, 2))
    parts, top, total, bias = call(
        own_forward_kernel,
        "own_forward",
        512,
        [(queries.shape, jnp.float32)] * 3 + [((rows, REACH * rows), jnp.float32)],
        lengths,
        here,
        queries,
        keys,
        values,
        scalars=2,
    )
    near_keys, near_values, bias = lax.optimization_barrier((keys, values, bias))
    for own, two, four in zip((near_keys, near_values), twos, fours):
        send = call(
            choose_kernel,
            "choose",
            0,
            [((rows, wide), jnp.bfloat16)],
            here,
            own,
            four,
            two,
            scalars=1,
        )[0]
        fars += [four, two, swapped(send)]
    out, dq_far, keep, two, four, odd = call(
        far_kernel,
        "far",
        6 * 1024,
        [
            (queries.shape, jnp.bfloat16),
            (queries.shape, jnp.bfloat16),
            ((rows, width), jnp.float32),
            ((rows, wide), jnp.float32),
            ((rows, wide), jnp.float32),
            ((rows, 2 * wide), jnp.bfloat16),
        ],
        queries,
        output_gradient,
        parts,
        top,
        total,
        bias,
        *fars,
        scratch=[pltpu.VMEM((groups, REACH * rows, width), jnp.bfloat16)] * 2
        + [pltpu.VMEM(queries.shape, jnp.bfloat16)] * 2
        + [pltpu.VMEM((rows, width), jnp.float32), pltpu.SemaphoreType.DMA((2 * groups + 1,))],
        hbm=(0, 1, 2),
    )
    other = swapped(odd)
    two, four = call(
        join_kernel,
        "join",
        0,
        [((rows, wide), jnp.bfloat16)] * 2,
        here,
        two,
        four,
        other,
        scalars=1,
    )
    two_back, four_back = up(two, -2), up(four, -4)
    split = lax.axis_size("head")
    got = lax.all_to_all(
        out.reshape(split, rows // split, out.shape[1]), "head", split_axis=0, concat_axis=0
    )
    keep, two = lax.optimization_barrier((keep, two))
    d_queries, own = call(
        own_backward_kernel,
        "own_backward",
        1024,
        [(queries.shape, jnp.bfloat16), ((rows, wide), jnp.float32)],
        lengths,
        here,
        queries,
        output_gradient,
        dq_far,
        keep,
        keys,
        values,
        scalars=2,
    )
    key_gradient, value_gradient = call(
        total_kernel,
        "total",
        0,
        [(keys.shape, jnp.bfloat16)] * 2,
        here,
        own,
        other,
        two_back,
        four_back,
        scalars=1,
    )
    attn_out = jnp.transpose(got, (1, 0, 2)).reshape(got.shape[1], -1)
    return (attn_out, d_queries, key_gradient, value_gradient)


def solution(mesh):
    placed = (P("seq", "head"), P("seq", "head"), P("seq", "head"), P("seq", "head"), P())
    return jax.shard_map(
        on_device,
        mesh=mesh,
        in_specs=placed,
        out_specs=(P(("seq", "head"), None), P("seq", "head"), P("seq", "head"), P("seq", "head")),
        check_vma=False,
    )
```

```python
import functools
import math

import jax
import jax.numpy as jnp
from jax import lax
from jax.experimental import pallas as pl
from jax.experimental.pallas import tpu as pltpu
from jax.sharding import PartitionSpec as P

HEAD_WIDTH = 128
REACH = 4
NEG = -1e30
LOG2E = 1.4426950408889634
PAIR = 2


def dot(a, b):
    return lax.dot_general(a, b, (((1,), (0,)), ((), ())), preferred_element_type=jnp.float32)


def dot_t(a, b):
    return lax.dot_general(a, b, (((1,), (1,)), ((), ())), preferred_element_type=jnp.float32)


def moved(value, to):
    count = lax.axis_size("seq")
    return lax.ppermute(value, "seq", [(source, to(source) % count) for source in range(count)])


def up(value, steps):
    return moved(value, lambda source: source + steps)


def swapped(value):
    return moved(value, lambda source: source ^ 1)


def first_seen(lens, here, rows, width):
    base = here[0] * rows
    row = lax.broadcasted_iota(jnp.int32, (rows, width), 0)

    def one(i, carry):
        end, start = carry
        end = end + lens[i]
        return end, jnp.where(row >= end - base, end - base, start)

    first = (jnp.int32(0), jnp.full((rows, width), -base, jnp.int32))
    return lax.fori_loop(0, lens.shape[0], one, first)[1]


def mask(start, distance):
    row = lax.broadcasted_iota(jnp.int32, start.shape, 0)
    pos = lax.broadcasted_iota(jnp.int32, start.shape, 1) - distance
    seen = pos >= start if distance >= start.shape[0] else (pos >= start) & (pos <= row)
    return jnp.where(seen, 0.0, NEG).astype(jnp.float32)


def near_mask(start, rows):
    width = start.shape[1]
    return jnp.concatenate([mask(start, -at) for at in range(0, rows, width)], axis=1)


def own_forward_kernel(
    scale, lens, here, q_ref, k_ref, v_ref, out_ref, top_ref, sum_ref, far_ref
):
    rows, width = q_ref.shape[0], HEAD_WIDTH
    start = first_seen(lens, here, rows, width)
    for at in range(0, REACH * rows, width):
        far_ref[:, at : at + width] = mask(start, REACH * rows - at)
    near = near_mask(start, rows)
    heads = q_ref.shape[1] // width
    share = q_ref.shape[1] // k_ref.shape[1]
    for h in range(heads):
        at = slice(h * width, (h + 1) * width)
        kv = slice(h // share * width, (h // share + 1) * width)
        s = dot_t(q_ref[:, at], k_ref[:, kv]) + near
        top = s.max(axis=1, keepdims=True)
        p = jnp.exp2((s - top) * (scale * LOG2E))
        top_ref[:, at] = jnp.broadcast_to(top, (rows, width))
        sum_ref[:, at] = jnp.broadcast_to(p.sum(axis=1, keepdims=True), (rows, width))
        out_ref[:, at] = dot(p.astype(jnp.bfloat16), v_ref[:, kv])


def far_kernel(scale, *refs):
    q_ref, g_ref, out_ref, top_ref, sum_ref, bias_ref = refs[0:6]
    (o_out, dq_out, keep_out, two_out, four_out, odd_out) = refs[-12:-6]
    k_all, v_all, o_ref, dq_ref, keep_ref, sent = refs[-6:]
    fars = refs[6:-12]
    rows, width = q_ref.shape[0], HEAD_WIDTH
    groups = k_all.shape[0]
    heads = q_ref.shape[1] // width
    share = heads // groups
    factor = scale * LOG2E
    bias = bias_ref[...]
    for which, to in enumerate((k_all, v_all)):
        two_ref, four_ref, odd_ref = fars[3 * which : 3 * which + 3]
        for b, (ref, place) in enumerate(((four_ref, 0), (odd_ref, 1), (two_ref, 0), (odd_ref, 0))):
            for n in range(groups):
                column = (groups * place + n) * width
                to[n, b * rows : (b + 1) * rows, :] = ref[:, column : column + width]

    def weigh(h):
        at = slice(h * width, (h + 1) * width)
        q, top = q_ref[:, at], top_ref[:, at]
        s = dot_t(q, k_all[h // share]) + bias
        most = jnp.maximum(top, s.max(axis=1, keepdims=True))
        p = jnp.exp2((s - jnp.tile(most, (1, s.shape[1] // width))) * factor)
        keep = jnp.exp2((top - most) * factor)
        total = sum_ref[:, at] * keep + p.sum(axis=1, keepdims=True)
        return at, q, p, most, keep, total

    def send(n):
        to = slice(n * share * width, (n + 1) * share * width)
        pairs = [(o_ref.at[:, to], o_out.at[:, to]), (dq_ref.at[:, to], dq_out.at[:, to])]
        if n == groups - 1:
            pairs.append((keep_ref, keep_out))
        return [pltpu.make_async_copy(*pair, sent.at[2 * n + i]) for i, pair in enumerate(pairs)]

    def settle(h, at, q, p, most, keep, total):
        inverse = 1.0 / total
        pb = p.astype(jnp.bfloat16)
        o = (dot(pb, v_all[h // share]) + out_ref[:, at] * keep) * inverse
        o_ref[:, at] = o.astype(jnp.bfloat16)
        gs = (g_ref[:, at].astype(jnp.float32) * inverse).astype(jnp.bfloat16)
        delta = jnp.sum(gs.astype(jnp.float32) * o, axis=1, keepdims=True)
        keep_ref[:, h : h + 1] = most[:, :1] * factor + jnp.log2(total[:, :1])
        keep_ref[:, heads + h : heads + h + 1] = delta * total[:, :1]
        return h, at, q, p, pb, gs, delta

    def differ(h, at, q, p, pb, gs, delta):
        ds = (p * (dot_t(gs, v_all[h // share]) - delta)).astype(jnp.bfloat16)
        dq_ref[:, at] = dot(ds, k_all[h // share]).astype(jnp.bfloat16)
        return q, gs, ds, pb

    weighed, settled, held = weigh(0), None, []
    for h in range(heads + 1):
        ahead = weigh(h + 1) if h + 1 < heads else None
        done = settle(h, *weighed) if h < heads else None
        if settled is not None:
            held.append(differ(*settled))
            if len(held) == PAIR:
                q, gs, ds, pb = (jnp.concatenate(x, axis=0) for x in zip(*held))
                held = []
                dk_part, dv_part = dot(q.T, ds), dot(gs.T, pb)
                if h % share == PAIR:
                    dk, dv = dk_part, dv_part
                else:
                    dk, dv = dk + dk_part, dv + dv_part
            if h % share == 0:
                n = h // share - 1
                for copy in send(n):
                    copy.start()
                outs = ((four_out, 0), (odd_out, 1), (two_out, 0), (odd_out, 0))
                for b, (ref, place) in enumerate(outs):
                    at = slice(b * rows, (b + 1) * rows)
                    for which, grad in enumerate((dk[:, at].T * scale, dv[:, at].T)):
                        to = (2 * groups * place + 2 * n + which) * width
                        ref[:, to : to + width] = grad.astype(ref.dtype)
        weighed, settled = ahead, done
    for n in range(groups):
        for copy in send(n):
            copy.wait()


def own_backward_kernel(
    scale, lens, here, q_ref, g_ref, far_ref, keep_ref, k_ref, v_ref, other_ref, dq_ref, own_ref
):
    rows, width = q_ref.shape[0], HEAD_WIDTH
    heads = q_ref.shape[1] // width
    share = q_ref.shape[1] // k_ref.shape[1]
    factor = scale * LOG2E
    bias = near_mask(first_seen(lens, here, rows, width), rows)
    one = jnp.where(here[0] % 2 == 0, 1.0, 0.0)
    for h in range(heads):
        n = h // share
        at = slice(h * width, (h + 1) * width)
        kv = slice(n * width, (n + 1) * width)
        k, v = k_ref[:, kv], v_ref[:, kv]
        q, g = q_ref[:, at], g_ref[:, at]
        p = jnp.exp2((dot_t(q, k) + bias) * factor - keep_ref[:, h : h + 1])
        ds = (p * (dot_t(g, v) - keep_ref[:, heads + h : heads + h + 1])).astype(jnp.bfloat16)
        dq = far_ref[:, at].astype(jnp.float32) + dot(ds, k)
        dq_ref[:, at] = (dq * scale).astype(jnp.bfloat16)
        dk_part, dv_part = dot(q.T, ds), dot(g.T, p.astype(jnp.bfloat16))
        dk, dv = (dk_part, dv_part) if h % share == 0 else (dk + dk_part, dv + dv_part)
        if h % share == share - 1:
            for which, grad in enumerate((dk.T * scale, dv.T)):
                to = slice((2 * n + which) * width, (2 * n + which + 1) * width)
                own_ref[:, to] = grad + other_ref[:, to].astype(jnp.float32) * one


def choose_kernel(scale, place, own_ref, two_ref, four_ref, send_ref):
    even = place[0] % 2 == 0
    half = own_ref.shape[1]

    @pl.when(even)
    def _():
        send_ref[:, :half] = own_ref[...]
        send_ref[:, half:] = two_ref[...]

    @pl.when(jnp.logical_not(even))
    def _():
        send_ref[:, :half] = two_ref[...]
        send_ref[:, half:] = four_ref[...]


def join_kernel(scale, place, two_ref, four_ref, other_ref, two_out, four_out):
    even = place[0] % 2 == 0
    half = two_ref.shape[1]

    @pl.when(even)
    def _():
        three = other_ref[:, half:].astype(jnp.float32)
        two_out[...] = (two_ref[...] + three).astype(jnp.bfloat16)
        four_out[...] = four_ref[...].astype(jnp.bfloat16)

    @pl.when(jnp.logical_not(even))
    def _():
        one = other_ref[:, :half].astype(jnp.float32)
        three = other_ref[:, half:].astype(jnp.float32)
        two_out[...] = (two_ref[...] + one).astype(jnp.bfloat16)
        four_out[...] = (four_ref[...] + three).astype(jnp.bfloat16)


def total_kernel(scale, own_ref, two_ref, four_ref, k_out, v_out):
    width = HEAD_WIDTH
    for n in range(k_out.shape[1] // width):
        for which, ref in enumerate((k_out, v_out)):
            at = slice((2 * n + which) * width, (2 * n + which + 1) * width)
            total = own_ref[:, at] + two_ref[:, at].astype(jnp.float32) + four_ref[:, at].astype(jnp.float32)
            ref[:, n * width : (n + 1) * width] = total.astype(jnp.bfloat16)


def call(kernel, name, cost, outs, *args, scalars=0, scratch=(), hbm=()):
    whole = pl.BlockSpec(memory_space=pltpu.VMEM)
    left = pl.BlockSpec(memory_space=pltpu.HBM)
    return pl.pallas_call(
        functools.partial(kernel, 1.0 / math.sqrt(HEAD_WIDTH)),
        in_specs=[pl.BlockSpec(memory_space=pltpu.SMEM)] * scalars + [whole] * (len(args) - scalars),
        out_specs=[left if i in hbm else whole for i in range(len(outs))],
        out_shape=[
            pltpu.HBM(shape, dtype) if i in hbm else jax.ShapeDtypeStruct(shape, dtype)
            for i, (shape, dtype) in enumerate(outs)
        ],
        scratch_shapes=scratch,
        compiler_params=pltpu.CompilerParams(vmem_limit_bytes=20 << 20),
        cost_estimate=pl.CostEstimate(
            flops=cost << 20, bytes_accessed=1 << 20, transcendentals=0
        ),
        name=name,
    )(*args)


def on_device(queries, keys, values, output_gradient, lengths):
    rows, width = queries.shape[0], HEAD_WIDTH
    groups = keys.shape[1] // width
    heads = queries.shape[1] // width
    wide = 2 * groups * width
    place = lax.axis_index("seq")
    here = place.reshape(1).astype(jnp.int32)
    twos, fours, fars = [], [], []
    for own in (keys, values):
        twos.append(up(own, 2))
        fours.append(up(own, 4))
    parts, top, total, bias = call(
        own_forward_kernel,
        "own_forward",
        512,
        [(queries.shape, jnp.float32)] * 3 + [((rows, REACH * rows), jnp.float32)],
        lengths,
        here,
        queries,
        keys,
        values,
        scalars=2,
    )
    near_keys, near_values, bias = lax.optimization_barrier((keys, values, bias))
    for own, two, four in zip((near_keys, near_values), twos, fours):
        send = call(
            choose_kernel,
            "choose",
            0,
            [((rows, wide), jnp.bfloat16)],
            here,
            own,
            two,
            four,
            scalars=1,
        )[0]
        fars += [two, four, swapped(send)]
    out, dq_far, keep, two, four, odd = call(
        far_kernel,
        "far",
        6 * 1024,
        [
            (queries.shape, jnp.bfloat16),
            (queries.shape, jnp.bfloat16),
            ((rows, width), jnp.float32),
            ((rows, wide), jnp.float32),
            ((rows, wide), jnp.float32),
            ((rows, 2 * wide), jnp.bfloat16),
        ],
        queries,
        output_gradient,
        parts,
        top,
        total,
        bias,
        *fars,
        scratch=[pltpu.VMEM((groups, REACH * rows, width), jnp.bfloat16)] * 2
        + [pltpu.VMEM(queries.shape, jnp.bfloat16)] * 2
        + [pltpu.VMEM((rows, width), jnp.float32), pltpu.SemaphoreType.DMA((2 * groups + 1,))],
        hbm=(0, 1, 2),
    )
    other = swapped(odd)
    two, four = call(
        join_kernel,
        "join",
        0,
        [((rows, wide), jnp.bfloat16)] * 2,
        here,
        two,
        four,
        other,
        scalars=1,
    )
    two_back, four_back = up(two, -2), up(four, -4)
    split = lax.axis_size("head")
    got = lax.all_to_all(
        out.reshape(split, rows // split, out.shape[1]), "head", split_axis=0, concat_axis=0
    )
    keep, two = lax.optimization_barrier((keep, two))
    d_queries, own = call(
        own_backward_kernel,
        "own_backward",
        1024,
        [(queries.shape, jnp.bfloat16), ((rows, wide), jnp.float32)],
        lengths,
        here,
        queries,
        output_gradient,
        dq_far,
        keep,
        keys,
        values,
        other,
        scalars=2,
    )
    key_gradient, value_gradient = call(
        total_kernel,
        "total",
        0,
        [(keys.shape, jnp.bfloat16)] * 2,
        own,
        two_back,
        four_back,
    )
    attn_out = jnp.transpose(got, (1, 0, 2)).reshape(got.shape[1], -1)
    return (attn_out, d_queries, key_gradient, value_gradient)


def solution(mesh):
    placed = (P("seq", "head"), P("seq", "head"), P("seq", "head"), P("seq", "head"), P())
    return jax.shard_map(
        on_device,
        mesh=mesh,
        in_specs=placed,
        out_specs=(P(("seq", "head"), None), P("seq", "head"), P("seq", "head"), P("seq", "head")),
        check_vma=False,
    )
```
